128 devices in a mesh: group: 8 (over y_lo, z), dev: 16 (over x, y_hi, core).
Axes of the slice: x: 4, y: 4 (y_hi: 2, y_lo: 2; y = y_hi * 2 + y_lo), z: 4, core: 2. Of those that a mesh axis runs over, the one named last changes fastest.
Arguments:
- field_now: float32 [2, 512, 512, 256], P(None, 'group', 'dev'), may hold values from -6 to 6
- source: float32 [2, 512, 512, 256], P(None, 'group', 'dev'), may hold values from -6 to 6
- wavenumber_sq: float32 [512, 512, 256], P('group', 'dev'), may hold values from 0.02 to 0.2
- shift_sq: float32 [1], replicated, may hold values from 0.05 to 0.2
Outputs:
- field_next: float32 [2, 512, 512, 256], P(None, 'group', 'dev')
The draws below stay inside these ranges and needn't reach their ends.
All inputs are finite; a program needn't handle non-finite values.
Results may differ from the reference program's by a relative error of at most 0.000092.
Values sent between devices are 32-bit elements; how exact they have to be, the bound alone decides.
A program may use at most 128 MiB of HBM per device.

```python
import math
import jax
import jax.numpy as jnp
from jax import lax

NZ = 256
SWEEPS = 3
NX = 512
NY = 512


def level_of(stream_key, shape, split, low, high):
    def one(position, shards_of):
        draws = jax.random.uniform(jax.random.fold_in(jax.random.fold_in(stream_key, 6), position), (shards_of,), jnp.float32, low / len(split), high / len(split))
        return jnp.repeat(jnp.exp(draws), shape[position] // shards_of).reshape((-1,) + (1,) * (len(shape) - position - 1))

    gain = one(*split[0])
    for cut in split[1:]:
        gain = gain * one(*cut)
    return gain


def bell_draw(key, dims, width, most, cuts=(), kind=jnp.bfloat16):
    loudness = level_of(key, dims, cuts, -0.22, 0.18) if cuts else 1.0
    result = jax.random.normal(key, dims, jnp.float32) * width * loudness
    return jnp.minimum(jnp.maximum(result, -most), most).astype(kind)


def setup_inputs(seed: int = 0) -> dict:
    key_of = jax.random.split(jax.random.key(seed), 5)
    return {
        "field_now": bell_draw(key_of[0], (2, NX, NY, NZ), 1.0, 6.0, ((1, 8), (2, 16)), jnp.float32),
        "source": bell_draw(key_of[1], (2, NX, NY, NZ), 1.0, 6.0, ((1, 8), (2, 16)), jnp.float32),
        "wavenumber_sq": jnp.clip(jnp.exp(math.log(0.2) - 2.3025851 * jax.random.uniform(key_of[2], (NX, NY, NZ), jnp.float32) ** level_of(key_of[2], (NX, NY, NZ), ((0, 8), (1, 16)), -0.2, 0.2)), 0.02, 0.2),
        "shift_sq": jnp.clip(jax.random.uniform(key_of[3], (1,), jnp.float32, 0.05, 0.2), 0.05, 0.2),
    }


RELAX = 0.8
DAMPING = 0.5
HIGHEST = lax.Precision.HIGHEST

def operate(padded, wave_sq):
    centre = padded[:, 1:-1, 1:-1, :]
    beside = padded[:, 2:, 1:-1, :] + padded[:, :-2, 1:-1, :]
    beside = beside + padded[:, 1:-1, 2:, :] + padded[:, 1:-1, :-2, :]
    vertical = jnp.pad(centre, ((0, 0), (0, 0), (0, 0), (1, 1)))
    beside = beside + vertical[..., 2:] + vertical[..., :-2]
    layers = centre.shape[-1]
    height = lax.broadcasted_iota(jnp.int32, (1, 1, layers), 2)
    boundary = jnp.logical_or(height == 0, height == layers - 1).astype(wave_sq.dtype)
    absorb = jnp.sqrt(wave_sq)
    robin = jnp.stack([centre[0] - absorb * centre[1], centre[1] + absorb * centre[0]]) * boundary
    return (6.0 - wave_sq) * centre - beside - robin

def fourier_table(count, sign, real_type):
    index_row = lax.broadcasted_iota(jnp.int32, (count, count), 0)
    index_col = lax.broadcasted_iota(jnp.int32, (count, count), 1)
    angle = 2.0 * math.pi / count * (index_row * index_col % count).astype(real_type)
    cosine = jnp.cos(angle)
    sine = sign * jnp.sin(angle)
    scale = 1.0 if sign < 0 else 1.0 / count
    return scale * jnp.stack([jnp.stack([cosine, sine]), jnp.stack([-sine, cosine])])

def vertical_basis(layers, real_type):
    index_row = lax.broadcasted_iota(jnp.int32, (layers, layers), 0) + 1
    index_col = lax.broadcasted_iota(jnp.int32, (layers, layers), 1) + 1
    angle = math.pi / (layers + 1) * (index_row * index_col % (2 * (layers + 1))).astype(real_type)
    return math.sqrt(2.0 / (layers + 1)) * jnp.sin(angle)

def horizontal_eigen(wave_index, count, real_type):
    angle = 2.0 * math.pi / count * wave_index.astype(real_type)
    return (2.0 - 2.0 * jnp.cos(angle)) / 16.0

def vertical_eigen(mode_index, layers, real_type):
    angle = math.pi / (layers + 1) * (mode_index + 1).astype(real_type)
    return 2.0 - 2.0 * jnp.cos(angle)

def divide_modes(modes, eigen, shift):
    real_part = eigen - shift
    imag_part = -DAMPING * shift
    modulus = real_part * real_part + imag_part * imag_part
    upper = (modes[0] * real_part + modes[1] * imag_part) / modulus
    lower = (modes[1] * real_part - modes[0] * imag_part) / modulus
    return jnp.stack([upper, lower])

def restrict(residual):
    extent = residual.shape
    blocks = residual.reshape(2, extent[1] // 4, 4, extent[2] // 4, 4, extent[3])
    return lax.optimization_barrier(jnp.mean(blocks, axis=(2, 4)))

def prolong(coarse):
    extent = coarse.shape
    spread = jnp.broadcast_to(coarse[:, :, None, :, None, :], (2, extent[1], 4, extent[2], 4, extent[3]))
    return spread.reshape(2, extent[1] * 4, extent[2] * 4, extent[3])

def coarse_solve(coarse, shift):
    real_type = coarse.dtype
    waves_x = coarse.shape[1]
    waves_y = coarse.shape[2]
    layers = coarse.shape[3]
    basis = vertical_basis(layers, real_type)
    modes = jnp.einsum('cxyz,zm->cmxy', coarse, basis, precision=HIGHEST)
    modes = jnp.einsum('cmxy,cdyk->dmxk', modes, fourier_table(waves_y, -1, real_type), precision=HIGHEST)
    modes = jnp.einsum('cmxk,cdxj->dmjk', modes, fourier_table(waves_x, -1, real_type), precision=HIGHEST)
    mode_index = lax.broadcasted_iota(jnp.int32, (layers, 1, 1), 0)
    wave_x = lax.broadcasted_iota(jnp.int32, (1, waves_x, 1), 1)
    wave_y = lax.broadcasted_iota(jnp.int32, (1, 1, waves_y), 2)
    eigen = vertical_eigen(mode_index, layers, real_type) + horizontal_eigen(wave_x, waves_x, real_type) + horizontal_eigen(wave_y, waves_y, real_type)
    modes = divide_modes(modes, eigen, shift)
    modes = jnp.einsum('cmjk,cdjx->dmxk', modes, fourier_table(waves_x, 1, real_type), precision=HIGHEST)
    modes = jnp.einsum('cmxk,cdky->dmxy', modes, fourier_table(waves_y, 1, real_type), precision=HIGHEST)
    return jnp.einsum('cmxy,mz->cxyz', modes, basis, precision=HIGHEST)

def reference(field_now, source, wavenumber_sq, shift_sq):
    padded = jnp.pad(field_now, ((0, 0), (1, 1), (1, 1), (0, 0)))
    residual = source - operate(padded, wavenumber_sq)
    correction = coarse_solve(restrict(residual), shift_sq[0])
    field = field_now + prolong(correction)
    weight = RELAX / (6.0 - wavenumber_sq)
    for sweep_index in range(SWEEPS):
        padded = jnp.pad(field, ((0, 0), (1, 1), (1, 1), (0, 0)))
        field = field + weight * (source - operate(padded, wavenumber_sq))
    return field
```

```python
import functools
import math

import jax
import jax.numpy as jnp
import numpy as np
from jax import lax
from jax.experimental import pallas as pl
from jax.experimental.pallas import tpu as pltpu
from jax.sharding import PartitionSpec as P

SWEEPS = 3
RELAX = 0.8
DAMPING = 0.5
HIGHEST = lax.Precision.HIGHEST
MESH = pl.DeviceIdType.MESH

GROUPS, MEMBERS = 8, 16
DEVICES = GROUPS * MEMBERS
LX, LY, NZ = 64, 32, 256
CX, CY = LX // 4, LY // 4
PAD_X, PAD_Y = LX + 2, LY + 16
LANES = 128
TILES = LY // 8
F32 = jnp.float32


def block_real(matrix):
    return np.block([[matrix.real, -matrix.imag], [matrix.imag, matrix.real]])


def tables():
    count = 128
    z = np.arange(NZ) + 1
    basis = math.sqrt(2.0 / (NZ + 1)) * np.sin(math.pi / (NZ + 1) * np.outer(z, z))

    def dft(n):
        return np.exp(-2j * math.pi * np.outer(np.arange(n), np.arange(n)) / n)

    rows = np.kron(dft(GROUPS), dft(MEMBERS))
    lanes = np.kron(dft(CX), dft(CY))
    j1, k1 = np.repeat(np.arange(GROUPS), MEMBERS), np.tile(np.arange(MEMBERS), GROUPS)
    xi, yi = np.repeat(np.arange(CX), CY), np.tile(np.arange(CY), CX)
    twiddle = np.exp(-2j * math.pi * (np.outer(j1, xi) + np.outer(k1, yi)) / count)
    j2, k2 = xi, yi
    wave_x = j1[:, None] + GROUPS * j2[None, :]
    wave_y = k1[:, None] + MEMBERS * k2[None, :]
    eigen = (2 - 2 * np.cos(2 * math.pi * wave_x / count)) / 16
    eigen = eigen + (2 - 2 * np.cos(2 * math.pi * wave_y / count)) / 16
    vertical = 2 - 2 * np.cos(math.pi * z / (NZ + 1))
    forward_rows = block_real(rows)
    forward_lanes = block_real(lanes).T
    floats = (
        basis,
        forward_rows,
        forward_lanes,
        forward_lanes.T / count,
        forward_rows.T / count,
        np.stack([twiddle.real, twiddle.imag]),
        eigen,
        vertical,
    )
    return [np.asarray(a, np.float32) for a in floats]


def dot(a, b, contract):
    return lax.dot_general(
        a, b, ((contract[:1], contract[1:]), ((), ())), precision=HIGHEST,
        preferred_element_type=F32,
    )


def stencil(field, x, tile, absorb, lane):
    low = 8 + 8 * tile
    centre = [field[hc, x + 1, low : low + 8, :] for hc in range(4)]
    total = []
    for hc in range(4):
        beside = field[hc, x, low : low + 8, :] + field[hc, x + 2, low : low + 8, :]
        beside = beside + field[hc, x + 1, low - 1 : low + 7, :]
        beside = beside + field[hc, x + 1, low + 1 : low + 9, :]
        total.append(beside)
    after = [pltpu.roll(v, 1, axis=1) for v in centre]
    before = [pltpu.roll(v, LANES - 1, axis=1) for v in centre]
    robin = [
        centre[0] - absorb * centre[2],
        centre[1] - absorb * centre[3],
        centre[2] + absorb * centre[0],
        centre[3] + absorb * centre[1],
    ]
    first, final = lane == 0, lane == LANES - 1
    for c in range(2):
        a, b = 2 * c, 2 * c + 1
        total[a] = total[a] + jnp.where(first, robin[a], after[a])
        total[a] = total[a] + jnp.where(final, before[b], before[a])
        total[b] = total[b] + jnp.where(first, after[a], after[b])
        total[b] = total[b] + jnp.where(final, robin[b], before[b])
    return centre, total


def kernel(
    f_hbm, s_hbm, k_hbm, shift_ref, vertical_ref,
    basis_ref, rows_ref, lanes_ref, unlanes_ref, unrows_ref, twiddle_ref, eigen_ref,
    out_hbm,
    fa, fb, src, wave, weight, absorb_ref, summed, coarse,
    send1, recv1, send2, recv2,
    sy, sx, ry, rx, sey, sex, rey, rex,
    load_sem, store_sem, a2a_sem, halo_send, halo_recv,
):
    g, d = lax.axis_index("group"), lax.axis_index("dev")
    me = g * MEMBERS + d

    loads = []
    for c in range(2):
        for h in range(2):
            z = pl.ds(LANES * h, LANES)
            loads.append(pltpu.make_async_copy(
                f_hbm.at[c, :, :, z], fa.at[2 * c + h, pl.ds(1, LX), pl.ds(8, LY), :],
                load_sem.at[2 * c + h]))
    for c in range(2):
        for h in range(2):
            z = pl.ds(LANES * h, LANES)
            loads.append(pltpu.make_async_copy(
                s_hbm.at[c, :, :, z], src.at[2 * c + h], load_sem.at[4 + 2 * c + h]))
    for h in range(2):
        loads.append(pltpu.make_async_copy(
            k_hbm.at[:, :, pl.ds(LANES * h, LANES)], wave.at[h], load_sem.at[8 + h]))
    for copy in loads:
        copy.start()

    for ref in (ry, rx, rey, rex):
        ref[...] = jnp.zeros_like(ref)

    barrier = pltpu.get_barrier_semaphore()

    def greet(i, carry):
        t = lax.rem(me + i, DEVICES)
        pl.semaphore_signal(
            barrier, inc=1, device_id=(t // MEMBERS, lax.rem(t, MEMBERS)), device_id_type=MESH)
        return carry

    lax.fori_loop(1, DEVICES, greet, 0)

    for ref in (fa, fb):
        ref[:, 0] = jnp.zeros((4, PAD_Y, LANES), F32)
        ref[:, PAD_X - 1] = jnp.zeros((4, PAD_Y, LANES), F32)

        def clear(x, carry, ref=ref):
            ref[:, x, 0:8, :] = jnp.zeros((4, 8, LANES), F32)
            ref[:, x, PAD_Y - 8 : PAD_Y, :] = jnp.zeros((4, 8, LANES), F32)
            return carry

        lax.fori_loop(1, PAD_X - 1, clear, 0)

    pl.semaphore_wait(barrier, DEVICES - 1)

    def sides(e, out_y, out_x, in_y, in_x):
        plan = []
        for side in range(2):
            step = 2 * side - 1
            for axis, (place, size, out, into) in enumerate(
                ((d, MEMBERS, out_y, in_y), (g, GROUPS, out_x, in_x))
            ):
                here = place > 0 if side == 0 else place < size - 1
                target = (g, d + step) if axis == 0 else (g + step, d)
                plan.append((
                    here,
                    pltpu.make_async_remote_copy(
                        src_ref=out.at[side], dst_ref=into.at[1 - side],
                        send_sem=halo_send.at[e, 2 * axis + side],
                        recv_sem=halo_recv.at[e, 2 * axis + 1 - side],
                        device_id=target, device_id_type=MESH),
                    pltpu.make_async_remote_copy(
                        src_ref=out.at[side], dst_ref=into.at[side],
                        send_sem=halo_send.at[e, 2 * axis + side],
                        recv_sem=halo_recv.at[e, 2 * axis + side],
                        device_id=target, device_id_type=MESH),
                ))
        return plan

    def start_sides(plan):
        for here, copy, _ in plan:
            pl.when(here)(copy.start)

    def finish_sides(plan):
        for here, _, arrived in plan:
            @pl.when(here)
            def _(arrived=arrived):
                arrived.wait_send()
                arrived.wait_recv()

    def pack(field, e):
        flat = field.reshape(4, PAD_X * PAD_Y, LANES)
        for hc in range(4):
            for side, row in ((0, 8), (1, 7 + LY)):
                sy[e, side, hc] = flat[hc, pl.ds(PAD_Y + row, LX, stride=PAD_Y), :]
            for side, x in ((0, 1), (1, LX)):
                sx[e, side, hc] = field[hc, x, 8 : 8 + LY, :]

    def beside(e):
        return sides(e, sy.at[e], sx.at[e], ry.at[e], rx.at[e])

    for copy in loads[:4]:
        copy.wait()
    pack(fa, 0)
    start = beside(0)
    start_sides(start)
    for copy in loads[4:]:
        copy.wait()

    lane = lax.broadcasted_iota(jnp.int32, (8, LANES), 1)
    sub = lax.broadcasted_iota(jnp.int32, (8, LANES), 0)

    def residual(xi, carry):
        for tile in range(TILES):
            rows = slice(8 * tile, 8 * tile + 8)
            sums = [None] * 4
            for q in range(4):
                x = 4 * xi + q
                k = [wave[h, x, rows, :] for h in range(2)]
                absorb = jnp.sqrt(jnp.where(lane < LANES // 2, k[0], k[1]))
                absorb_ref[x, rows, :] = absorb
                diagonal = [6.0 - v for v in k]
                for h in range(2):
                    weight[h, x, rows, :] = RELAX / diagonal[h]
                centre, total = stencil(fa, x, tile, absorb, lane)
                for hc in range(4):
                    value = src[hc, x, rows, :] + total[hc] - diagonal[hc % 2] * centre[hc]
                    sums[hc] = value if q == 0 else sums[hc] + value
            for hc in range(4):
                summed[hc, pl.ds(pl.multiple_of(xi * LY + 8 * tile, 8), 8), :] = sums[hc]
        return carry

    lax.fori_loop(0, CX, residual, 0)

    finish_sides(start)
    cells = CX * CY
    for hc in range(4):
        value = summed[hc, pl.ds(0, cells, stride=4), :]
        for q in range(1, 4):
            value = value + summed[hc, pl.ds(q, cells, stride=4), :]
        coarse[hc] = value
        for side in range(2):
            for q in range(4):
                at = pl.ds(7 * side, CX, stride=CY)
                coarse[hc, at, :] = coarse[hc, at, :] + ry[0, side, hc, pl.ds(q, CX, stride=4), :]
            for q in range(4):
                at = pl.ds((CX - 1) * CY * side, CY)
                coarse[hc, at, :] = coarse[hc, at, :] + rx[0, side, hc, pl.ds(q, CY, stride=4), :]

    mean = jnp.concatenate(
        [jnp.concatenate([coarse[0], coarse[1]], axis=1),
         jnp.concatenate([coarse[2], coarse[3]], axis=1)], axis=0) * (1.0 / 16.0)
    modes = dot(basis_ref[...], mean, (1, 1))
    send1_flat = send1.reshape(4 * DEVICES, LANES)
    for m in range(2):
        for c in range(2):
            send1_flat[pl.ds(2 * m + c, DEVICES, stride=4), :] = modes[
                DEVICES * m : DEVICES * (m + 1), LANES * c : LANES * (c + 1)]

    def to_all(source, target, index):
        def one(i, carry):
            t = lax.rem(me + i, DEVICES)
            pltpu.make_async_remote_copy(
                src_ref=source.at[t], dst_ref=target.at[me],
                send_sem=a2a_sem.at[2 * index], recv_sem=a2a_sem.at[2 * index + 1],
                device_id=(t // MEMBERS, lax.rem(t, MEMBERS)), device_id_type=MESH).start()
            return carry

        lax.fori_loop(1, DEVICES, one, 0)
        target[me] = source[me]
        some = pl.ds(0, DEVICES - 1)
        pltpu.make_async_copy(source.at[some], source.at[some], a2a_sem.at[2 * index]).wait()
        pltpu.make_async_copy(target.at[some], target.at[some], a2a_sem.at[2 * index + 1]).wait()

    to_all(send1, recv1, 0)

    recv1_flat = recv1.reshape(4 * DEVICES, LANES)
    part = [recv1_flat[pl.ds(q, DEVICES, stride=4), :] for q in range(4)]
    planes = jnp.concatenate(
        [jnp.concatenate([part[0], part[2]], axis=1),
         jnp.concatenate([part[1], part[3]], axis=1)], axis=0)
    planes = dot(rows_ref[...], planes, (1, 0))
    cosine, sine = twiddle_ref[0], twiddle_ref[1]

    def quarter(value, row, column):
        return value[LANES * row : LANES * (row + 1), LANES * column : LANES * (column + 1)]

    turned = []
    for m in range(2):
        real, imag = quarter(planes, 0, m), quarter(planes, 1, m)
        turned.append(jnp.concatenate(
            [real * cosine - imag * sine, real * sine + imag * cosine], axis=1))
    planes = dot(jnp.concatenate(turned, axis=0), lanes_ref[...], (1, 0))
    shift = shift_ref[0]
    imag_part = -DAMPING * shift
    solved = []
    for m in range(2):
        real, imag = quarter(planes, m, 0), quarter(planes, m, 1)
        real_part = eigen_ref[...] + (vertical_ref[me + DEVICES * m] - shift)
        modulus = real_part * real_part + imag_part * imag_part
        upper = (real * real_part + imag * imag_part) / modulus
        lower = (imag * real_part - real * imag_part) / modulus
        solved.append(jnp.concatenate([upper, lower], axis=1))
    planes = dot(jnp.concatenate(solved, axis=0), unlanes_ref[...], (1, 0))
    turned = [[], []]
    for m in range(2):
        real, imag = quarter(planes, m, 0), quarter(planes, m, 1)
        turned[0].append(real * cosine + imag * sine)
        turned[1].append(imag * cosine - real * sine)
    planes = dot(
        unrows_ref[...],
        jnp.concatenate([jnp.concatenate(row, axis=1) for row in turned], axis=0), (1, 0))
    send2_flat = send2.reshape(4 * DEVICES, LANES)
    for m in range(2):
        for c in range(2):
            send2_flat[pl.ds(2 * m + c, DEVICES, stride=4), :] = quarter(planes, c, m)

    to_all(send2, recv2, 1)

    recv2_flat = recv2.reshape(4 * DEVICES, LANES)
    part = [recv2_flat[pl.ds(q, DEVICES, stride=4), :] for q in range(4)]
    modes = jnp.concatenate(
        [jnp.concatenate([part[0], part[1]], axis=1),
         jnp.concatenate([part[2], part[3]], axis=1)], axis=0)
    correction = dot(modes, basis_ref[...], (0, 0))
    for c in range(2):
        for h in range(2):
            coarse[2 * c + h] = quarter(correction, c, h)

    for hc in range(4):
        for side in range(2):
            sey[side, hc] = coarse[hc, pl.ds(7 * side, CX, stride=CY), :]
            sex[side, hc] = coarse[hc, pl.ds((CX - 1) * CY * side, CY), :]
    edges = sides(3, sey, sex, rey, rex)
    start_sides(edges)

    def prolong(xi, carry):
        for tile in range(TILES):
            row = xi * CY + 2 * tile
            for hc in range(4):
                lower = jnp.broadcast_to(coarse[hc, pl.ds(row, 1), :], (8, LANES))
                upper = jnp.broadcast_to(coarse[hc, pl.ds(row + 1, 1), :], (8, LANES))
                spread = jnp.where(sub < 4, lower, upper)
                for q in range(4):
                    x = 4 * xi + q + 1
                    at = slice(8 + 8 * tile, 16 + 8 * tile)
                    fa[hc, x, at, :] = fa[hc, x, at, :] + spread
        return carry

    lax.fori_loop(0, CX, prolong, 0)

    def sweep(old, new):
        def one(x, carry):
            for tile in range(TILES):
                rows = slice(8 * tile, 8 * tile + 8)
                centre, total = stencil(old, x, tile, absorb_ref[x, rows, :], lane)
                for hc in range(4):
                    value = weight[hc % 2, x, rows, :] * (src[hc, x, rows, :] + total[hc])
                    new[hc, x + 1, 8 + 8 * tile : 16 + 8 * tile, :] = (
                        (1.0 - RELAX) * centre[hc] + value)
            return carry

        lax.fori_loop(0, LX, one, 0)

    def add_halos(new, e):
        flat = new.reshape(4, PAD_X * PAD_Y, LANES)
        scale = weight.reshape(2, LX * LY, LANES)
        for hc in range(4):
            h = hc % 2
            for side, row in ((0, 0), (1, LY - 1)):
                at = pl.ds(PAD_Y + 8 + row, LX, stride=PAD_Y)
                flat[hc, at, :] = flat[hc, at, :] + (
                    scale[h, pl.ds(row, LX, stride=LY), :] * ry[e, side, hc])
            for side, x in ((0, 0), (1, LX - 1)):
                new[hc, x + 1, 8 : 8 + LY, :] = new[hc, x + 1, 8 : 8 + LY, :] + (
                    weight[h, x] * rx[e, side, hc])

    sweep(fa, fb)
    finish_sides(edges)
    for hc in range(4):
        for side in range(2):
            for q in range(4):
                at = pl.ds(q, CX, stride=4)
                ry[0, side, hc, at, :] = ry[0, side, hc, at, :] + rey[side, hc]
                at = pl.ds(q, CY, stride=4)
                rx[0, side, hc, at, :] = rx[0, side, hc, at, :] + rex[side, hc]
    add_halos(fb, 0)
    for e, old, new in ((1, fb, fa), (2, fa, fb)):
        pack(old, e)
        plan = beside(e)
        start_sides(plan)
        sweep(old, new)
        finish_sides(plan)
        add_halos(new, e)

    stores = []
    for c in range(2):
        for h in range(2):
            stores.append(pltpu.make_async_copy(
                fb.at[2 * c + h, pl.ds(1, LX), pl.ds(8, LY), :],
                out_hbm.at[c, :, :, pl.ds(LANES * h, LANES)], store_sem.at[2 * c + h]))
    for copy in stores:
        copy.start()
    for copy in stores:
        copy.wait()


def body(field_now, source, wavenumber_sq, shift_sq):
    basis, rows, lanes, unlanes, unrows, twiddle, eigen, vertical = tables()
    anywhere = pl.BlockSpec(memory_space=pl.ANY)
    scalars = pl.BlockSpec(memory_space=pltpu.SMEM)
    whole = pl.BlockSpec(memory_space=pltpu.VMEM)
    vmem = pltpu.VMEM
    dma = pltpu.SemaphoreType.DMA
    return pl.pallas_call(
        kernel,
        out_shape=jax.ShapeDtypeStruct(field_now.shape, F32),
        in_specs=[anywhere] * 3 + [scalars] * 2 + [whole] * 7,
        out_specs=anywhere,
        scratch_shapes=[
            vmem((4, PAD_X, PAD_Y, LANES), F32),
            vmem((4, PAD_X, PAD_Y, LANES), F32),
            vmem((4, LX, LY, LANES), F32),
            vmem((2, LX, LY, LANES), F32),
            vmem((2, LX, LY, LANES), F32),
            vmem((LX, LY, LANES), F32),
            vmem((4, CX * LY, LANES), F32),
            vmem((4, CX * CY, LANES), F32),
            vmem((DEVICES, 4, LANES), F32),
            vmem((DEVICES, 4, LANES), F32),
            vmem((DEVICES, 4, LANES), F32),
            vmem((DEVICES, 4, LANES), F32),
            vmem((3, 2, 4, LX, LANES), F32),
            vmem((3, 2, 4, LY, LANES), F32),
            vmem((3, 2, 4, LX, LANES), F32),
            vmem((3, 2, 4, LY, LANES), F32),
            vmem((2, 4, CX, LANES), F32),
            vmem((2, 4, CY, LANES), F32),
            vmem((2, 4, CX, LANES), F32),
            vmem((2, 4, CY, LANES), F32),
            dma((10,)),
            dma((4,)),
            dma((4,)),
            dma((4, 4)),
            dma((4, 4)),
        ],
        compiler_params=pltpu.CompilerParams(
            collective_id=0, has_side_effects=True, vmem_limit_bytes=48 << 20),
        name="schwarz",
    )(field_now, source, wavenumber_sq, shift_sq, vertical,
      basis, rows, lanes, unlanes, unrows, twiddle, eigen)


def solution(mesh):
    return jax.shard_map(
        body,
        mesh=mesh,
        in_specs=(
            P(None, "group", "dev", None),
            P(None, "group", "dev", None),
            P("group", "dev", None),
            P(),
        ),
        out_specs=P(None, "group", "dev", None),
        check_vma=False,
    )
```

```python
import functools
import math

import jax
import jax.numpy as jnp
import numpy as np
from jax import lax
from jax.experimental import pallas as pl
from jax.experimental.pallas import tpu as pltpu
from jax.sharding import PartitionSpec as P

SWEEPS = 3
UNROLL = 4
LIMIT = 67043328
RELAX = 0.8
DAMPING = 0.5
HIGHEST = lax.Precision.HIGHEST
MESH = pl.DeviceIdType.MESH

GROUPS, MEMBERS = 8, 16
DEVICES = GROUPS * MEMBERS
LX, LY, NZ = 64, 32, 256
CX, CY = LX // 4, LY // 4
PARTS = 4
PAD_X, PAD_Y = LX + 2, LY + 16
LANES = 128
TILES = LY // 8
F32 = jnp.float32


def block_real(matrix):
    return np.block([[matrix.real, -matrix.imag], [matrix.imag, matrix.real]])


def tables():
    count = 128
    z = np.arange(NZ) + 1
    basis = math.sqrt(2.0 / (NZ + 1)) * np.sin(math.pi / (NZ + 1) * np.outer(z, z))

    def dft(n):
        return np.exp(-2j * math.pi * np.outer(np.arange(n), np.arange(n)) / n)

    rows = np.kron(dft(GROUPS), dft(MEMBERS))
    lanes = np.kron(dft(CX), dft(CY))
    j1, k1 = np.repeat(np.arange(GROUPS), MEMBERS), np.tile(np.arange(MEMBERS), GROUPS)
    xi, yi = np.repeat(np.arange(CX), CY), np.tile(np.arange(CY), CX)
    twiddle = np.exp(-2j * math.pi * (np.outer(j1, xi) + np.outer(k1, yi)) / count)
    j2, k2 = xi, yi
    wave_x = j1[:, None] + GROUPS * j2[None, :]
    wave_y = k1[:, None] + MEMBERS * k2[None, :]
    eigen = (2 - 2 * np.cos(2 * math.pi * wave_x / count)) / 16
    eigen = eigen + (2 - 2 * np.cos(2 * math.pi * wave_y / count)) / 16
    vertical = 2 - 2 * np.cos(math.pi * z / (NZ + 1))
    forward_rows = block_real(rows)
    forward_lanes = block_real(lanes).T
    wide = [basis, forward_rows, forward_lanes, forward_lanes.T / count, forward_rows.T / count]
    narrow = [twiddle.real, twiddle.imag, eigen, np.tile(vertical[:, None], (1, LANES))]
    return np.float32(np.stack(wide)), np.float32(np.concatenate(narrow))


def dot(a, b, contract):
    return lax.dot_general(
        a, b, ((contract[:1], contract[1:]), ((), ())), precision=HIGHEST,
        preferred_element_type=F32,
    )


def stencil(field, x, tile, absorb, lane):
    low = 8 + 8 * tile
    centre = [field[hc, x + 1, low : low + 8, :] for hc in range(4)]
    total = []
    for hc in range(4):
        beside = field[hc, x, low : low + 8, :] + field[hc, x + 2, low : low + 8, :]
        beside = beside + field[hc, x + 1, low - 1 : low + 7, :]
        beside = beside + field[hc, x + 1, low + 1 : low + 9, :]
        total.append(beside)
    after = [pltpu.roll(v, 1, axis=1) for v in centre]
    before = [pltpu.roll(v, LANES - 1, axis=1) for v in centre]
    robin = [
        centre[0] - absorb * centre[2],
        centre[1] - absorb * centre[3],
        centre[2] + absorb * centre[0],
        centre[3] + absorb * centre[1],
    ]
    first, final = lane == 0, lane == LANES - 1
    for c in range(2):
        a, b = 2 * c, 2 * c + 1
        total[a] = total[a] + jnp.where(first, robin[a], after[a])
        total[a] = total[a] + jnp.where(final, before[b], before[a])
        total[b] = total[b] + jnp.where(first, after[a], after[b])
        total[b] = total[b] + jnp.where(final, robin[b], before[b])
    return centre, total


def kernel(
    f_hbm, s_hbm, k_hbm, shift_ref, wide_hbm, narrow_hbm,
    out_hbm, edge_y_hbm, edge_x_hbm,
    fa, fb, res, edge_y, edge_x, src, wave, weight, absorb_ref, summed, coarse, wide, narrow,
    send1, recv1, send2, recv2,
    sy, sx, ry, rx, sey, sex, rey, rex,
    load_sem, part_sem, table_sem, a2a_sem, halo_send, halo_recv, store_sem, ready,
):
    g, d = lax.axis_index("group"), lax.axis_index("dev")
    me = g * MEMBERS + d

    barrier = pltpu.get_barrier_semaphore()

    column = [lax.rem(d + j, MEMBERS) for j in range(MEMBERS)]

    def everyone(start):
        def row(i, carry):
            tg = lax.rem(g + i, GROUPS)
            for td in column:
                start(tg, td)
            return carry

        lax.fori_loop(1, GROUPS, row, 0)
        for td in column[1:]:
            start(g, td)

    for ref in (ry, rx, rey, rex):
        ref[...] = jnp.zeros_like(ref)

    for i in range(1, GROUPS):
        pl.semaphore_signal(
            barrier, inc=1, device_id=(lax.rem(g + i, GROUPS), d), device_id_type=MESH)
    for td in column[1:]:
        pl.semaphore_signal(barrier, inc=1, device_id=(g, td), device_id_type=MESH)

    halves = [pl.ds(LANES * h, LANES) for h in range(2)]
    loads = []
    for hc in range(4):
        loads.append(pltpu.make_async_copy(
            f_hbm.at[hc // 2, :, :, halves[hc % 2]],
            fa.at[hc, pl.ds(1, LX), pl.ds(8, LY), :], load_sem.at[hc]))
    for copy in loads:
        copy.start()

    def part_loads(i):
        x = pl.ds(i * (LX // PARTS), LX // PARTS)
        copies = []
        for hc in range(4):
            copies.append(pltpu.make_async_copy(
                s_hbm.at[hc // 2, x, :, halves[hc % 2]], src.at[hc, x], part_sem.at[i, hc]))
        for h in range(2):
            copies.append(pltpu.make_async_copy(
                k_hbm.at[x, :, halves[h]], wave.at[h, x], part_sem.at[i, 4 + h]))
        return copies

    for i in range(PARTS):
        for copy in part_loads(i):
            copy.start()
    constants = [
        pltpu.make_async_copy(wide_hbm, wide, table_sem.at[0]),
        pltpu.make_async_copy(narrow_hbm, narrow, table_sem.at[1]),
    ]
    for copy in constants:
        copy.start()

    for ref in (fa, fb):
        ref[:, 0] = jnp.zeros((4, PAD_Y, LANES), F32)
        ref[:, PAD_X - 1] = jnp.zeros((4, PAD_Y, LANES), F32)

        def clear(x, carry, ref=ref):
            ref[:, x, 0:8, :] = jnp.zeros((4, 8, LANES), F32)
            ref[:, x, PAD_Y - 8 : PAD_Y, :] = jnp.zeros((4, 8, LANES), F32)
            return carry

        lax.fori_loop(1, PAD_X - 1, clear, 0)

    pl.semaphore_wait(barrier, GROUPS + MEMBERS - 2)
    for i in range(1, GROUPS):
        pl.semaphore_signal(
            ready, inc=1, device_id=(lax.rem(g + i, GROUPS), d), device_id_type=MESH)

    def sides(e, out_y, out_x, in_y, in_x):
        plan = []
        for side in range(2):
            step = 2 * side - 1
            for axis, (place, size, out, into) in enumerate(
                ((d, MEMBERS, out_y, in_y), (g, GROUPS, out_x, in_x))
            ):
                here = place > 0 if side == 0 else place < size - 1
                target = (g, d + step) if axis == 0 else (g + step, d)
                plan.append((
                    here,
                    pltpu.make_async_remote_copy(
                        src_ref=out.at[side], dst_ref=into.at[1 - side],
                        send_sem=halo_send.at[e, 2 * axis + side],
                        recv_sem=halo_recv.at[e, 2 * axis + 1 - side],
                        device_id=target, device_id_type=MESH),
                    pltpu.make_async_remote_copy(
                        src_ref=out.at[side], dst_ref=into.at[side],
                        send_sem=halo_send.at[e, 2 * axis + side],
                        recv_sem=halo_recv.at[e, 2 * axis + side],
                        device_id=target, device_id_type=MESH),
                ))
        return plan

    def start_sides(plan):
        for here, copy, _ in plan:
            pl.when(here)(copy.start)

    def finish_sides(plan):
        for here, _, arrived in plan:
            @pl.when(here)
            def _(arrived=arrived):
                arrived.wait_send()
                arrived.wait_recv()

    def pack(field, e):
        flat = field.reshape(4, PAD_X * PAD_Y, LANES)
        for hc in range(4):
            for side, row in ((0, 8), (1, 7 + LY)):
                sy[e, side, hc] = flat[hc, pl.ds(PAD_Y + row, LX, stride=PAD_Y), :]
            for side, x in ((0, 1), (1, LX)):
                sx[e, side, hc] = field[hc, x, 8 : 8 + LY, :]

    def beside(e):
        return sides(e, sy.at[e], sx.at[e], ry.at[e], rx.at[e])

    for copy in loads:
        copy.wait()
    pack(fa, 0)
    start = beside(0)
    start_sides(start)

    lane = lax.broadcasted_iota(jnp.int32, (8, LANES), 1)
    sub = lax.broadcasted_iota(jnp.int32, (8, LANES), 0)

    def residual(xi, carry):
        for tile in range(TILES):
            rows = slice(8 * tile, 8 * tile + 8)
            sums = [None] * 4
            for q in range(4):
                x = 4 * xi + q
                k = [wave[h, x, rows, :] for h in range(2)]
                absorb = jnp.sqrt(jnp.where(lane < LANES // 2, k[0], k[1]))
                absorb_ref[x, rows, :] = absorb
                diagonal = [6.0 - v for v in k]
                for h in range(2):
                    weight[h, x, rows, :] = RELAX / diagonal[h]
                centre, total = stencil(fa, x, tile, absorb, lane)
                for hc in range(4):
                    value = src[hc, x, rows, :] + total[hc] - diagonal[hc % 2] * centre[hc]
                    sums[hc] = value if q == 0 else sums[hc] + value
            for hc in range(4):
                summed[hc, pl.ds(pl.multiple_of(xi * LY + 8 * tile, 8), 8), :] = sums[hc]
        return carry

    def residual_part(i, carry):
        for copy in part_loads(i):
            copy.wait()
        return lax.fori_loop(i * (CX // PARTS), (i + 1) * (CX // PARTS), residual, carry)

    lax.fori_loop(0, PARTS, residual_part, 0)
    for copy in constants:
        copy.wait()

    finish_sides(start)
    cells = CX * CY
    for hc in range(4):
        value = summed[hc, pl.ds(0, cells, stride=4), :]
        for q in range(1, 4):
            value = value + summed[hc, pl.ds(q, cells, stride=4), :]
        coarse[hc] = value
        for side in range(2):
            for q in range(4):
                at = pl.ds(7 * side, CX, stride=CY)
                coarse[hc, at, :] = coarse[hc, at, :] + ry[0, side, hc, pl.ds(q, CX, stride=4), :]
            for q in range(4):
                at = pl.ds((CX - 1) * CY * side, CY)
                coarse[hc, at, :] = coarse[hc, at, :] + rx[0, side, hc, pl.ds(q, CY, stride=4), :]

    mean = jnp.concatenate(
        [jnp.concatenate([coarse[0], coarse[1]], axis=1),
         jnp.concatenate([coarse[2], coarse[3]], axis=1)], axis=0) * (1.0 / 16.0)
    modes = dot(wide[0], mean, (1, 1))
    send1_flat = send1.reshape(4 * DEVICES, LANES)
    for m in range(2):
        for c in range(2):
            send1_flat[pl.ds(2 * m + c, DEVICES, stride=4), :] = modes[
                DEVICES * m : DEVICES * (m + 1), LANES * c : LANES * (c + 1)]

    def to_all(source, target, index):

        def one(tg, td):
            pltpu.make_async_remote_copy(
                src_ref=source.at[tg * MEMBERS + td], dst_ref=target.at[me],
                send_sem=a2a_sem.at[2 * index], recv_sem=a2a_sem.at[2 * index + 1],
                device_id=(tg, td), device_id_type=MESH).start()

        everyone(one)
        target[me] = source[me]
        some = pl.ds(0, DEVICES - 1)
        pltpu.make_async_copy(source.at[some], source.at[some], a2a_sem.at[2 * index]).wait()
        pltpu.make_async_copy(target.at[some], target.at[some], a2a_sem.at[2 * index + 1]).wait()

    pl.semaphore_wait(ready, GROUPS - 1)
    to_all(send1, recv1, 0)

    recv1_flat = recv1.reshape(4 * DEVICES, LANES)
    part = [recv1_flat[pl.ds(q, DEVICES, stride=4), :] for q in range(4)]
    planes = jnp.concatenate(
        [jnp.concatenate([part[0], part[2]], axis=1),
         jnp.concatenate([part[1], part[3]], axis=1)], axis=0)
    planes = dot(wide[1], planes, (1, 0))
    cosine, sine = narrow[0:LANES], narrow[LANES : 2 * LANES]

    def quarter(value, row, column):
        return value[LANES * row : LANES * (row + 1), LANES * column : LANES * (column + 1)]

    turned = []
    for m in range(2):
        real, imag = quarter(planes, 0, m), quarter(planes, 1, m)
        turned.append(jnp.concatenate(
            [real * cosine - imag * sine, real * sine + imag * cosine], axis=1))
    planes = dot(jnp.concatenate(turned, axis=0), wide[2], (1, 0))
    shift = shift_ref[0]
    imag_part = -DAMPING * shift
    solved = []
    for m in range(2):
        real, imag = quarter(planes, m, 0), quarter(planes, m, 1)
        height = narrow[pl.ds(3 * LANES + me + DEVICES * m, 1), :]
        real_part = narrow[2 * LANES : 3 * LANES] + (height - shift)
        modulus = real_part * real_part + imag_part * imag_part
        upper = (real * real_part + imag * imag_part) / modulus
        lower = (imag * real_part - real * imag_part) / modulus
        solved.append(jnp.concatenate([upper, lower], axis=1))
    planes = dot(jnp.concatenate(solved, axis=0), wide[3], (1, 0))
    turned = [[], []]
    for m in range(2):
        real, imag = quarter(planes, m, 0), quarter(planes, m, 1)
        turned[0].append(real * cosine + imag * sine)
        turned[1].append(imag * cosine - real * sine)
    planes = dot(
        wide[4],
        jnp.concatenate([jnp.concatenate(row, axis=1) for row in turned], axis=0), (1, 0))
    send2_flat = send2.reshape(4 * DEVICES, LANES)
    for m in range(2):
        for c in range(2):
            send2_flat[pl.ds(2 * m + c, DEVICES, stride=4), :] = quarter(planes, c, m)

    to_all(send2, recv2, 1)

    recv2_flat = recv2.reshape(4 * DEVICES, LANES)
    part = [recv2_flat[pl.ds(q, DEVICES, stride=4), :] for q in range(4)]
    modes = jnp.concatenate(
        [jnp.concatenate([part[0], part[1]], axis=1),
         jnp.concatenate([part[2], part[3]], axis=1)], axis=0)
    correction = dot(modes, wide[0], (0, 0))
    for c in range(2):
        for h in range(2):
            coarse[2 * c + h] = quarter(correction, c, h)

    for hc in range(4):
        for side in range(2):
            sey[side, hc] = coarse[hc, pl.ds(7 * side, CX, stride=CY), :]
            sex[side, hc] = coarse[hc, pl.ds((CX - 1) * CY * side, CY), :]
    edges = sides(3, sey, sex, rey, rex)
    start_sides(edges)

    def prolong(xi, carry):
        for tile in range(TILES):
            row = xi * CY + 2 * tile
            for hc in range(4):
                lower = jnp.broadcast_to(coarse[hc, pl.ds(row, 1), :], (8, LANES))
                upper = jnp.broadcast_to(coarse[hc, pl.ds(row + 1, 1), :], (8, LANES))
                spread = jnp.where(sub < 4, lower, upper)
                for q in range(4):
                    x = 4 * xi + q + 1
                    at = slice(8 + 8 * tile, 16 + 8 * tile)
                    fa[hc, x, at, :] = fa[hc, x, at, :] + spread
        return carry

    lax.fori_loop(0, CX, prolong, 0)

    def sweep(old, put, after=None):
        def some(i, carry):
            for tile in range(TILES):
                rows = slice(8 * tile, 8 * tile + 8)
                results = []
                for u in range(UNROLL):
                    x = UNROLL * i + u
                    centre, total = stencil(old, x, tile, absorb_ref[x, rows, :], lane)
                    for hc in range(4):
                        value = weight[hc % 2, x, rows, :] * (src[hc, x, rows, :] + total[hc])
                        results.append((hc, x, (1.0 - RELAX) * centre[hc] + value))
                for hc, x, value in results:
                    put(hc, x, tile, value)
            return carry

        steps = LX // UNROLL // PARTS

        def part(i, carry):
            lax.fori_loop(i * steps, (i + 1) * steps, some, carry)
            if after is not None:
                after(i)
            return carry

        lax.fori_loop(0, PARTS, part, 0)

    def into(field):
        def put(hc, x, tile, value):
            field[hc, x + 1, 8 + 8 * tile : 16 + 8 * tile, :] = value

        return put

    def put_out(hc, x, tile, value):
        res[hc, x, 8 * tile : 8 * tile + 8, :] = value

    def stores(i):
        x = pl.ds(i * (LX // PARTS), LX // PARTS)
        return [pltpu.make_async_copy(res.at[hc, x], out_hbm.at[hc, x], store_sem.at[i, hc])
                for hc in range(4)]

    def start_stores(i):
        for copy in stores(i):
            copy.start()

    def add_halos(new, e):
        flat = new.reshape(4, PAD_X * PAD_Y, LANES)
        scale = weight.reshape(2, LX * LY, LANES)
        for hc in range(4):
            h = hc % 2
            for side, row in ((0, 0), (1, LY - 1)):
                at = pl.ds(PAD_Y + 8 + row, LX, stride=PAD_Y)
                flat[hc, at, :] = flat[hc, at, :] + (
                    scale[h, pl.ds(row, LX, stride=LY), :] * ry[e, side, hc])
            for side, x in ((0, 0), (1, LX - 1)):
                new[hc, x + 1, 8 : 8 + LY, :] = new[hc, x + 1, 8 : 8 + LY, :] + (
                    weight[h, x] * rx[e, side, hc])

    sweep(fa, into(fb))
    finish_sides(edges)
    for hc in range(4):
        for side in range(2):
            for q in range(4):
                at = pl.ds(q, CX, stride=4)
                ry[0, side, hc, at, :] = ry[0, side, hc, at, :] + rey[side, hc]
                at = pl.ds(q, CY, stride=4)
                rx[0, side, hc, at, :] = rx[0, side, hc, at, :] + rex[side, hc]
    add_halos(fb, 0)
    pack(fb, 1)
    plan = beside(1)
    start_sides(plan)
    sweep(fb, into(fa))
    finish_sides(plan)
    add_halos(fa, 1)
    pack(fa, 2)
    plan = beside(2)
    start_sides(plan)
    sweep(fa, put_out, start_stores)
    finish_sides(plan)
    scale = weight.reshape(2, LX * LY, LANES)
    for hc in range(4):
        h = hc % 2
        for side, row in ((0, 0), (1, LY - 1)):
            edge_y[side, hc] = scale[h, pl.ds(row, LX, stride=LY), :] * ry[2, side, hc]
        for side, x in ((0, 0), (1, LX - 1)):
            edge_x[side, hc] = weight[h, x] * rx[2, side, hc]
    last = [
        pltpu.make_async_copy(edge_y, edge_y_hbm, table_sem.at[0]),
        pltpu.make_async_copy(edge_x, edge_x_hbm, table_sem.at[1]),
    ]
    for copy in last:
        copy.start()
    for i in range(PARTS):
        for copy in stores(i):
            copy.wait()
    for copy in last:
        copy.wait()


def finish(parts, edge_y_hbm, edge_x_hbm, out_hbm, field, edge_y, edge_x, sem_in, sem_edge, sem_out):
    edges = [
        pltpu.make_async_copy(edge_y_hbm, edge_y, sem_edge.at[0]),
        pltpu.make_async_copy(edge_x_hbm, edge_x, sem_edge.at[1]),
    ]
    half = LX // 2
    blocks = [(hc, i) for hc in range(4) for i in range(2)]
    loads = [
        pltpu.make_async_copy(
            parts.at[hc, pl.ds(half * i, half)], field.at[hc, pl.ds(half * i, half)],
            sem_in.at[hc, i])
        for hc, i in blocks
    ]
    stores = [
        pltpu.make_async_copy(
            field.at[hc, pl.ds(half * i, half)],
            out_hbm.at[hc // 2, pl.ds(half * i, half), :, pl.ds(LANES * (hc % 2), LANES)],
            sem_out.at[hc, i])
        for hc, i in blocks
    ]
    for copy in edges + loads:
        copy.start()
    for copy in edges:
        copy.wait()
    flat = field.reshape(4, LX * LY, LANES)
    for (hc, i), load, store in zip(blocks, loads, stores):
        load.wait()
        for side, row in ((0, 0), (1, LY - 1)):
            at = pl.ds(half * i * LY + row, half, stride=LY)
            flat[hc, at, :] = flat[hc, at, :] + edge_y[side, hc, half * i : half * (i + 1), :]
        x = (LX - 1) * i
        field[hc, x] = field[hc, x] + edge_x[i, hc]
        store.start()
    for store in stores:
        store.wait()


def body(field_now, source, wavenumber_sq, shift_sq):
    wide, narrow = tables()
    hbm = pl.BlockSpec(memory_space=pltpu.HBM)
    vmem = pltpu.VMEM
    dma = pltpu.SemaphoreType.DMA
    edges = [(2, 4, LX, LANES), (2, 4, LY, LANES)]
    parts = pl.pallas_call(
        kernel,
        out_shape=[jax.ShapeDtypeStruct(s, F32) for s in [(4, LX, LY, LANES)] + edges],
        in_specs=[hbm] * 3 + [pl.BlockSpec(memory_space=pltpu.SMEM)] + [hbm] * 2,
        out_specs=[hbm] * 3,
        scratch_shapes=[
            vmem((4, PAD_X, PAD_Y, LANES), F32),
            vmem((4, PAD_X, PAD_Y, LANES), F32),
            vmem((4, LX, LY, LANES), F32),
            vmem(edges[0], F32),
            vmem(edges[1], F32),
            vmem((4, LX, LY, LANES), F32),
            vmem((2, LX, LY, LANES), F32),
            vmem((2, LX, LY, LANES), F32),
            vmem((LX, LY, LANES), F32),
            vmem((4, CX * LY, LANES), F32),
            vmem((4, CX * CY, LANES), F32),
            vmem(wide.shape, F32),
            vmem(narrow.shape, F32),
        ] + [vmem((DEVICES, 4, LANES), F32)] * 4 + [
            vmem((3, 2, 4, LX, LANES), F32),
            vmem((3, 2, 4, LY, LANES), F32),
            vmem((3, 2, 4, LX, LANES), F32),
            vmem((3, 2, 4, LY, LANES), F32),
            vmem((2, 4, CX, LANES), F32),
            vmem((2, 4, CY, LANES), F32),
            vmem((2, 4, CX, LANES), F32),
            vmem((2, 4, CY, LANES), F32),
            dma((4,)),
            dma((PARTS, 6)),
            dma((2,)),
            dma((4,)),
            dma((4, 4)),
            dma((4, 4)),
            dma((PARTS, 4)),
            pltpu.SemaphoreType.REGULAR,
        ],
        compiler_params=pltpu.CompilerParams(
            collective_id=0, has_side_effects=True, vmem_limit_bytes=LIMIT),
        name="schwarz",
    )(field_now, source, wavenumber_sq, shift_sq, wide, narrow)
    return pl.pallas_call(
        finish,
        out_shape=jax.ShapeDtypeStruct(field_now.shape, F32),
        in_specs=[hbm] * 3,
        out_specs=hbm,
        scratch_shapes=[
            vmem((4, LX, LY, LANES), F32),
            vmem(edges[0], F32),
            vmem(edges[1], F32),
            dma((4, 2)),
            dma((2,)),
            dma((4, 2)),
        ],
        compiler_params=pltpu.CompilerParams(vmem_limit_bytes=LIMIT),
        name="finish",
    )(*parts)


def solution(mesh):
    return jax.shard_map(
        body,
        mesh=mesh,
        in_specs=(
            P(None, "group", "dev", None),
            P(None, "group", "dev", None),
            P("group", "dev", None),
            P(),
        ),
        out_specs=P(None, "group", "dev", None),
        check_vma=False,
    )
```

```python
import functools
import math

import jax
import jax.numpy as jnp
import numpy as np
from jax import lax
from jax.experimental import pallas as pl
from jax.experimental.pallas import tpu as pltpu
from jax.sharding import PartitionSpec as P

SWEEPS = 3
UNROLL = 4
LIMIT = 67043328
RELAX = 0.8
DAMPING = 0.5
HIGHEST = lax.Precision.HIGHEST
MESH = pl.DeviceIdType.MESH

GROUPS, MEMBERS = 8, 16
DEVICES = GROUPS * MEMBERS
LX, LY, NZ = 64, 32, 256
CX, CY = LX // 4, LY // 4
PARTS = 4
PAD_X, PAD_Y = LX + 2, LY + 16
LANES = 128
TILES = LY // 8
F32 = jnp.float32


def block_real(matrix):
    return np.block([[matrix.real, -matrix.imag], [matrix.imag, matrix.real]])


def tables():
    count = 128
    z = np.arange(NZ) + 1
    basis = math.sqrt(2.0 / (NZ + 1)) * np.sin(math.pi / (NZ + 1) * np.outer(z, z))

    def dft(n):
        return np.exp(-2j * math.pi * np.outer(np.arange(n), np.arange(n)) / n)

    rows = np.kron(dft(GROUPS), dft(MEMBERS))
    lanes = np.kron(dft(CX), dft(CY))
    j1, k1 = np.repeat(np.arange(GROUPS), MEMBERS), np.tile(np.arange(MEMBERS), GROUPS)
    xi, yi = np.repeat(np.arange(CX), CY), np.tile(np.arange(CY), CX)
    twiddle = np.exp(-2j * math.pi * (np.outer(j1, xi) + np.outer(k1, yi)) / count)
    j2, k2 = xi, yi
    wave_x = j1[:, None] + GROUPS * j2[None, :]
    wave_y = k1[:, None] + MEMBERS * k2[None, :]
    eigen = (2 - 2 * np.cos(2 * math.pi * wave_x / count)) / 16
    eigen = eigen + (2 - 2 * np.cos(2 * math.pi * wave_y / count)) / 16
    vertical = 2 - 2 * np.cos(math.pi * z / (NZ + 1))
    forward_rows = block_real(rows)
    forward_lanes = block_real(lanes).T
    wide = [basis, forward_rows, forward_lanes, forward_lanes.T / count, forward_rows.T / count]
    narrow = [twiddle.real, twiddle.imag, eigen, np.tile(vertical[:, None], (1, LANES))]
    return np.float32(np.stack(wide)), np.float32(np.concatenate(narrow))


def dot(a, b, contract):
    return lax.dot_general(
        a, b, ((contract[:1], contract[1:]), ((), ())), precision=HIGHEST,
        preferred_element_type=F32,
    )


def stencil(field, x, tile, absorb, lane):
    low = 8 + 8 * tile
    centre = [field[hc, x + 1, low : low + 8, :] for hc in range(4)]
    total = []
    for hc in range(4):
        beside = field[hc, x, low : low + 8, :] + field[hc, x + 2, low : low + 8, :]
        beside = beside + field[hc, x + 1, low - 1 : low + 7, :]
        beside = beside + field[hc, x + 1, low + 1 : low + 9, :]
        total.append(beside)
    after = [pltpu.roll(v, 1, axis=1) for v in centre]
    before = [pltpu.roll(v, LANES - 1, axis=1) for v in centre]
    robin = [
        centre[0] - absorb * centre[2],
        centre[1] - absorb * centre[3],
        centre[2] + absorb * centre[0],
        centre[3] + absorb * centre[1],
    ]
    first, final = lane == 0, lane == LANES - 1
    for c in range(2):
        a, b = 2 * c, 2 * c + 1
        total[a] = total[a] + jnp.where(first, robin[a], after[a])
        total[a] = total[a] + jnp.where(final, before[b], before[a])
        total[b] = total[b] + jnp.where(first, after[a], after[b])
        total[b] = total[b] + jnp.where(final, robin[b], before[b])
    return centre, total


def kernel(
    f_hbm, s_hbm, k_hbm, shift_ref, wide_hbm, narrow_hbm,
    out_hbm, edge_y_hbm, edge_x_hbm,
    fa, fb, res, edge_y, edge_x, src, wave, weight, absorb_ref, summed, coarse, wide, narrow,
    send1, recv1, send2, recv2,
    sy, sx, ry, rx, sey, sex, rey, rex,
    load_sem, part_sem, table_sem, a2a_sem, halo_send, halo_recv, store_sem, ready,
):
    g, d = lax.axis_index("group"), lax.axis_index("dev")
    me = g * MEMBERS + d

    barrier = pltpu.get_barrier_semaphore()

    column = [lax.rem(d + j, MEMBERS) for j in range(MEMBERS)]

    def everyone(start):
        order = [(2, 1), (1, 1), (3, 1), (2, 0), (0, 1), (1, 0), (3, 0), (0, 0)]
        columns = [
            4 * lax.rem(d // 4 + c, 4) + 2 * lax.rem(d // 2 + e, 2) + lax.rem(d + f, 2)
            for c, e in order for f in (1, 0)
        ]

        def row(i, carry):
            i = i + i // 5
            tg = 4 * lax.rem(g // 4 + 1 + i, 2) + lax.rem(g + 2 + 3 * (i // 2), 4)
            for td in columns:
                start(tg, td)
            return carry

        lax.fori_loop(0, GROUPS - 1, row, 0)
        for td in columns[:-1]:
            start(g, td)

    for ref in (ry, rx, rey, rex):
        ref[...] = jnp.zeros_like(ref)

    for i in range(1, GROUPS):
        pl.semaphore_signal(
            barrier, inc=1, device_id=(lax.rem(g + i, GROUPS), d), device_id_type=MESH)
    for td in column[1:]:
        pl.semaphore_signal(barrier, inc=1, device_id=(g, td), device_id_type=MESH)

    halves = [pl.ds(LANES * h, LANES) for h in range(2)]
    loads = []
    for hc in range(4):
        loads.append(pltpu.make_async_copy(
            f_hbm.at[hc // 2, :, :, halves[hc % 2]],
            fa.at[hc, pl.ds(1, LX), pl.ds(8, LY), :], load_sem.at[hc]))
    for copy in loads:
        copy.start()

    def part_loads(i):
        x = pl.ds(i * (LX // PARTS), LX // PARTS)
        copies = []
        for hc in range(4):
            copies.append(pltpu.make_async_copy(
                s_hbm.at[hc // 2, x, :, halves[hc % 2]], src.at[hc, x], part_sem.at[i, hc]))
        for h in range(2):
            copies.append(pltpu.make_async_copy(
                k_hbm.at[x, :, halves[h]], wave.at[h, x], part_sem.at[i, 4 + h]))
        return copies

    for i in range(PARTS):
        for copy in part_loads(i):
            copy.start()
    constants = [
        pltpu.make_async_copy(wide_hbm, wide, table_sem.at[0]),
        pltpu.make_async_copy(narrow_hbm, narrow, table_sem.at[1]),
    ]
    for copy in constants:
        copy.start()

    for ref in (fa, fb):
        ref[:, 0] = jnp.zeros((4, PAD_Y, LANES), F32)
        ref[:, PAD_X - 1] = jnp.zeros((4, PAD_Y, LANES), F32)

        def clear(x, carry, ref=ref):
            ref[:, x, 0:8, :] = jnp.zeros((4, 8, LANES), F32)
            ref[:, x, PAD_Y - 8 : PAD_Y, :] = jnp.zeros((4, 8, LANES), F32)
            return carry

        lax.fori_loop(1, PAD_X - 1, clear, 0)

    pl.semaphore_wait(barrier, GROUPS + MEMBERS - 2)
    for i in range(1, GROUPS):
        pl.semaphore_signal(
            ready, inc=1, device_id=(lax.rem(g + i, GROUPS), d), device_id_type=MESH)

    def sides(e, out_y, out_x, in_y, in_x):
        plan = []
        for side in range(2):
            step = 2 * side - 1
            for axis, (place, size, out, into) in enumerate(
                ((d, MEMBERS, out_y, in_y), (g, GROUPS, out_x, in_x))
            ):
                here = place > 0 if side == 0 else place < size - 1
                target = (g, d + step) if axis == 0 else (g + step, d)
                plan.append((
                    here,
                    pltpu.make_async_remote_copy(
                        src_ref=out.at[side], dst_ref=into.at[1 - side],
                        send_sem=halo_send.at[e, 2 * axis + side],
                        recv_sem=halo_recv.at[e, 2 * axis + 1 - side],
                        device_id=target, device_id_type=MESH),
                    pltpu.make_async_remote_copy(
                        src_ref=out.at[side], dst_ref=into.at[side],
                        send_sem=halo_send.at[e, 2 * axis + side],
                        recv_sem=halo_recv.at[e, 2 * axis + side],
                        device_id=target, device_id_type=MESH),
                ))
        return plan

    def start_sides(plan):
        for here, copy, _ in plan:
            pl.when(here)(copy.start)

    sent = []

    def finish_sides(plan):
        for here, _, arrived in plan:
            pl.when(here)(arrived.wait_recv)
            sent.append((here, arrived.wait_send))

    def pack(field, e):
        flat = field.reshape(4, PAD_X * PAD_Y, LANES)
        for hc in range(4):
            for side, row in ((0, 8), (1, 7 + LY)):
                sy[e, side, hc] = flat[hc, pl.ds(PAD_Y + row, LX, stride=PAD_Y), :]
            for side, x in ((0, 1), (1, LX)):
                sx[e, side, hc] = field[hc, x, 8 : 8 + LY, :]

    def beside(e):
        return sides(e, sy.at[e], sx.at[e], ry.at[e], rx.at[e])

    for copy in loads:
        copy.wait()
    pack(fa, 0)
    for hc in range(4):
        for side in range(2):
            sey[0, side, hc] = sum(
                sy[0, side, hc, pl.ds(q, CX, stride=4), :] for q in range(4))
            sex[0, side, hc] = sum(
                sx[0, side, hc, pl.ds(q, CY, stride=4), :] for q in range(4))
    sums = sides(4, sey.at[0], sex.at[0], rey.at[0], rex.at[0])
    start_sides(sums)
    start = beside(0)
    start_sides(start)

    lane = lax.broadcasted_iota(jnp.int32, (8, LANES), 1)
    sub = lax.broadcasted_iota(jnp.int32, (8, LANES), 0)

    def residual(xi, carry):
        for tile in range(TILES):
            rows = slice(8 * tile, 8 * tile + 8)
            sums = [None] * 4
            for q in range(4):
                x = 4 * xi + q
                k = [wave[h, x, rows, :] for h in range(2)]
                absorb = jnp.sqrt(jnp.where(lane < LANES // 2, k[0], k[1]))
                absorb_ref[x, rows, :] = absorb
                diagonal = [6.0 - v for v in k]
                for h in range(2):
                    weight[h, x, rows, :] = RELAX / diagonal[h]
                centre, total = stencil(fa, x, tile, absorb, lane)
                for hc in range(4):
                    value = src[hc, x, rows, :] + total[hc] - diagonal[hc % 2] * centre[hc]
                    sums[hc] = value if q == 0 else sums[hc] + value
            for hc in range(4):
                summed[hc, pl.ds(pl.multiple_of(xi * LY + 8 * tile, 8), 8), :] = sums[hc]
        return carry

    def residual_part(i, carry):
        for copy in part_loads(i):
            copy.wait()
        return lax.fori_loop(i * (CX // PARTS), (i + 1) * (CX // PARTS), residual, carry)

    lax.fori_loop(0, PARTS, residual_part, 0)
    for copy in constants:
        copy.wait()

    finish_sides(sums)
    cells = CX * CY
    for hc in range(4):
        value = summed[hc, pl.ds(0, cells, stride=4), :]
        for q in range(1, 4):
            value = value + summed[hc, pl.ds(q, cells, stride=4), :]
        coarse[hc] = value
        for side in range(2):
            at = pl.ds(7 * side, CX, stride=CY)
            coarse[hc, at, :] = coarse[hc, at, :] + rey[0, side, hc]
            at = pl.ds((CX - 1) * CY * side, CY)
            coarse[hc, at, :] = coarse[hc, at, :] + rex[0, side, hc]

    mean = jnp.concatenate(
        [jnp.concatenate([coarse[0], coarse[1]], axis=1),
         jnp.concatenate([coarse[2], coarse[3]], axis=1)], axis=0) * (1.0 / 16.0)
    modes = dot(wide[0], mean, (1, 1))
    send1_flat = send1.reshape(4 * DEVICES, LANES)
    for m in range(2):
        for c in range(2):
            send1_flat[pl.ds(2 * m + c, DEVICES, stride=4), :] = modes[
                DEVICES * m : DEVICES * (m + 1), LANES * c : LANES * (c + 1)]

    def to_all(source, target, index):

        def one(tg, td):
            pltpu.make_async_remote_copy(
                src_ref=source.at[tg * MEMBERS + td], dst_ref=target.at[me],
                send_sem=a2a_sem.at[2 * index], recv_sem=a2a_sem.at[2 * index + 1],
                device_id=(tg, td), device_id_type=MESH).start()

        everyone(one)
        target[me] = source[me]
        some = pl.ds(0, DEVICES - 1)
        sent.append((None, pltpu.make_async_copy(
            source.at[some], source.at[some], a2a_sem.at[2 * index]).wait))
        pltpu.make_async_copy(target.at[some], target.at[some], a2a_sem.at[2 * index + 1]).wait()

    pl.semaphore_wait(ready, GROUPS - 1)
    to_all(send1, recv1, 0)

    recv1_flat = recv1.reshape(4 * DEVICES, LANES)
    part = [recv1_flat[pl.ds(q, DEVICES, stride=4), :] for q in range(4)]
    planes = jnp.concatenate(
        [jnp.concatenate([part[0], part[2]], axis=1),
         jnp.concatenate([part[1], part[3]], axis=1)], axis=0)
    planes = dot(wide[1], planes, (1, 0))
    cosine, sine = narrow[0:LANES], narrow[LANES : 2 * LANES]

    def quarter(value, row, column):
        return value[LANES * row : LANES * (row + 1), LANES * column : LANES * (column + 1)]

    turned = []
    for m in range(2):
        real, imag = quarter(planes, 0, m), quarter(planes, 1, m)
        turned.append(jnp.concatenate(
            [real * cosine - imag * sine, real * sine + imag * cosine], axis=1))
    planes = dot(jnp.concatenate(turned, axis=0), wide[2], (1, 0))
    shift = shift_ref[0]
    imag_part = -DAMPING * shift
    solved = []
    for m in range(2):
        real, imag = quarter(planes, m, 0), quarter(planes, m, 1)
        height = narrow[pl.ds(3 * LANES + me + DEVICES * m, 1), :]
        real_part = narrow[2 * LANES : 3 * LANES] + (height - shift)
        modulus = real_part * real_part + imag_part * imag_part
        upper = (real * real_part + imag * imag_part) / modulus
        lower = (imag * real_part - real * imag_part) / modulus
        solved.append(jnp.concatenate([upper, lower], axis=1))
    planes = dot(jnp.concatenate(solved, axis=0), wide[3], (1, 0))
    turned = [[], []]
    for m in range(2):
        real, imag = quarter(planes, m, 0), quarter(planes, m, 1)
        turned[0].append(real * cosine + imag * sine)
        turned[1].append(imag * cosine - real * sine)
    planes = dot(
        wide[4],
        jnp.concatenate([jnp.concatenate(row, axis=1) for row in turned], axis=0), (1, 0))
    send2_flat = send2.reshape(4 * DEVICES, LANES)
    for m in range(2):
        for c in range(2):
            send2_flat[pl.ds(2 * m + c, DEVICES, stride=4), :] = quarter(planes, c, m)

    to_all(send2, recv2, 1)

    recv2_flat = recv2.reshape(4 * DEVICES, LANES)
    part = [recv2_flat[pl.ds(q, DEVICES, stride=4), :] for q in range(4)]
    modes = jnp.concatenate(
        [jnp.concatenate([part[0], part[1]], axis=1),
         jnp.concatenate([part[2], part[3]], axis=1)], axis=0)
    correction = dot(modes, wide[0], (0, 0))
    for c in range(2):
        for h in range(2):
            coarse[2 * c + h] = quarter(correction, c, h)

    for hc in range(4):
        for side in range(2):
            sey[1, side, hc] = coarse[hc, pl.ds(7 * side, CX, stride=CY), :]
            sex[1, side, hc] = coarse[hc, pl.ds((CX - 1) * CY * side, CY), :]
    edges = sides(3, sey.at[1], sex.at[1], rey.at[1], rex.at[1])
    start_sides(edges)

    def prolong(xi, carry):
        for tile in range(TILES):
            row = xi * CY + 2 * tile
            for hc in range(4):
                lower = jnp.broadcast_to(coarse[hc, pl.ds(row, 1), :], (8, LANES))
                upper = jnp.broadcast_to(coarse[hc, pl.ds(row + 1, 1), :], (8, LANES))
                spread = jnp.where(sub < 4, lower, upper)
                for q in range(4):
                    x = 4 * xi + q + 1
                    at = slice(8 + 8 * tile, 16 + 8 * tile)
                    fa[hc, x, at, :] = fa[hc, x, at, :] + spread
        return carry

    lax.fori_loop(0, CX, prolong, 0)

    def sweep(old, put, after=None):
        def some(i, carry):
            for tile in range(TILES):
                rows = slice(8 * tile, 8 * tile + 8)
                results = []
                for u in range(UNROLL):
                    x = UNROLL * i + u
                    centre, total = stencil(old, x, tile, absorb_ref[x, rows, :], lane)
                    for hc in range(4):
                        value = weight[hc % 2, x, rows, :] * (src[hc, x, rows, :] + total[hc])
                        results.append((hc, x, (1.0 - RELAX) * centre[hc] + value))
                for hc, x, value in results:
                    put(hc, x, tile, value)
            return carry

        steps = LX // UNROLL // PARTS

        def part(i, carry):
            lax.fori_loop(i * steps, (i + 1) * steps, some, carry)
            if after is not None:
                after(i)
            return carry

        lax.fori_loop(0, PARTS, part, 0)

    def into(field):
        def put(hc, x, tile, value):
            field[hc, x + 1, 8 + 8 * tile : 16 + 8 * tile, :] = value

        return put

    def put_out(hc, x, tile, value):
        res[hc, x, 8 * tile : 8 * tile + 8, :] = value

    def stores(i):
        x = pl.ds(i * (LX // PARTS), LX // PARTS)
        return [pltpu.make_async_copy(res.at[hc, x], out_hbm.at[hc, x], store_sem.at[i, hc])
                for hc in range(4)]

    def start_stores(i):
        for copy in stores(i):
            copy.start()

    def add_halos(new, e):
        flat = new.reshape(4, PAD_X * PAD_Y, LANES)
        scale = weight.reshape(2, LX * LY, LANES)
        for hc in range(4):
            h = hc % 2
            for side, row in ((0, 0), (1, LY - 1)):
                at = pl.ds(PAD_Y + 8 + row, LX, stride=PAD_Y)
                flat[hc, at, :] = flat[hc, at, :] + (
                    scale[h, pl.ds(row, LX, stride=LY), :] * ry[e, side, hc])
            for side, x in ((0, 0), (1, LX - 1)):
                new[hc, x + 1, 8 : 8 + LY, :] = new[hc, x + 1, 8 : 8 + LY, :] + (
                    weight[h, x] * rx[e, side, hc])

    sweep(fa, into(fb))
    finish_sides(start)
    finish_sides(edges)
    for hc in range(4):
        for side in range(2):
            for q in range(4):
                at = pl.ds(q, CX, stride=4)
                ry[0, side, hc, at, :] = ry[0, side, hc, at, :] + rey[1, side, hc]
                at = pl.ds(q, CY, stride=4)
                rx[0, side, hc, at, :] = rx[0, side, hc, at, :] + rex[1, side, hc]
    add_halos(fb, 0)
    pack(fb, 1)
    plan = beside(1)
    start_sides(plan)
    sweep(fb, into(fa))
    finish_sides(plan)
    add_halos(fa, 1)
    pack(fa, 2)
    plan = beside(2)
    start_sides(plan)
    sweep(fa, put_out, start_stores)
    finish_sides(plan)
    scale = weight.reshape(2, LX * LY, LANES)
    for hc in range(4):
        h = hc % 2
        for side, row in ((0, 0), (1, LY - 1)):
            edge_y[side, hc] = scale[h, pl.ds(row, LX, stride=LY), :] * ry[2, side, hc]
        for side, x in ((0, 0), (1, LX - 1)):
            edge_x[side, hc] = weight[h, x] * rx[2, side, hc]
    last = [
        pltpu.make_async_copy(edge_y, edge_y_hbm, table_sem.at[0]),
        pltpu.make_async_copy(edge_x, edge_x_hbm, table_sem.at[1]),
    ]
    for copy in last:
        copy.start()
    for here, wait in sent:
        if here is None:
            wait()
        else:
            pl.when(here)(wait)
    for i in range(PARTS):
        for copy in stores(i):
            copy.wait()
    for copy in last:
        copy.wait()


def finish(parts, edge_y_hbm, edge_x_hbm, out_hbm, field, edge_y, edge_x, sem_in, sem_edge, sem_out):
    edges = [
        pltpu.make_async_copy(edge_y_hbm, edge_y, sem_edge.at[0]),
        pltpu.make_async_copy(edge_x_hbm, edge_x, sem_edge.at[1]),
    ]
    half = LX // 2
    blocks = [(hc, i) for hc in range(4) for i in range(2)]
    loads = [
        pltpu.make_async_copy(
            parts.at[hc, pl.ds(half * i, half)], field.at[hc, pl.ds(half * i, half)],
            sem_in.at[hc, i])
        for hc, i in blocks
    ]
    stores = [
        pltpu.make_async_copy(
            field.at[hc, pl.ds(half * i, half)],
            out_hbm.at[hc // 2, pl.ds(half * i, half), :, pl.ds(LANES * (hc % 2), LANES)],
            sem_out.at[hc, i])
        for hc, i in blocks
    ]
    for copy in edges + loads:
        copy.start()
    for copy in edges:
        copy.wait()
    flat = field.reshape(4, LX * LY, LANES)
    for (hc, i), load, store in zip(blocks, loads, stores):
        load.wait()
        for side, row in ((0, 0), (1, LY - 1)):
            at = pl.ds(half * i * LY + row, half, stride=LY)
            flat[hc, at, :] = flat[hc, at, :] + edge_y[side, hc, half * i : half * (i + 1), :]
        x = (LX - 1) * i
        field[hc, x] = field[hc, x] + edge_x[i, hc]
        store.start()
    for store in stores:
        store.wait()


def body(field_now, source, wavenumber_sq, shift_sq):
    wide, narrow = tables()
    hbm = pl.BlockSpec(memory_space=pltpu.HBM)
    vmem = pltpu.VMEM
    dma = pltpu.SemaphoreType.DMA
    edges = [(2, 4, LX, LANES), (2, 4, LY, LANES)]
    parts = pl.pallas_call(
        kernel,
        out_shape=[jax.ShapeDtypeStruct(s, F32) for s in [(4, LX, LY, LANES)] + edges],
        in_specs=[hbm] * 3 + [pl.BlockSpec(memory_space=pltpu.SMEM)] + [hbm] * 2,
        out_specs=[hbm] * 3,
        scratch_shapes=[
            vmem((4, PAD_X, PAD_Y, LANES), F32),
            vmem((4, PAD_X, PAD_Y, LANES), F32),
            vmem((4, LX, LY, LANES), F32),
            vmem(edges[0], F32),
            vmem(edges[1], F32),
            vmem((4, LX, LY, LANES), F32),
            vmem((2, LX, LY, LANES), F32),
            vmem((2, LX, LY, LANES), F32),
            vmem((LX, LY, LANES), F32),
            vmem((4, CX * LY, LANES), F32),
            vmem((4, CX * CY, LANES), F32),
            vmem(wide.shape, F32),
            vmem(narrow.shape, F32),
        ] + [vmem((DEVICES, 4, LANES), F32)] * 4 + [
            vmem((3, 2, 4, LX, LANES), F32),
            vmem((3, 2, 4, LY, LANES), F32),
            vmem((3, 2, 4, LX, LANES), F32),
            vmem((3, 2, 4, LY, LANES), F32),
            vmem((2, 2, 4, CX, LANES), F32),
            vmem((2, 2, 4, CY, LANES), F32),
            vmem((2, 2, 4, CX, LANES), F32),
            vmem((2, 2, 4, CY, LANES), F32),
            dma((4,)),
            dma((PARTS, 6)),
            dma((2,)),
            dma((4,)),
            dma((5, 4)),
            dma((5, 4)),
            dma((PARTS, 4)),
            pltpu.SemaphoreType.REGULAR,
        ],
        compiler_params=pltpu.CompilerParams(
            collective_id=0, has_side_effects=True, vmem_limit_bytes=LIMIT),
        name="schwarz",
    )(field_now, source, wavenumber_sq, shift_sq, wide, narrow)
    return pl.pallas_call(
        finish,
        out_shape=jax.ShapeDtypeStruct(field_now.shape, F32),
        in_specs=[hbm] * 3,
        out_specs=hbm,
        scratch_shapes=[
            vmem((4, LX, LY, LANES), F32),
            vmem(edges[0], F32),
            vmem(edges[1], F32),
            dma((4, 2)),
            dma((2,)),
            dma((4, 2)),
        ],
        compiler_params=pltpu.CompilerParams(vmem_limit_bytes=LIMIT),
        name="finish",
    )(*parts)


def solution(mesh):
    return jax.shard_map(
        body,
        mesh=mesh,
        in_specs=(
            P(None, "group", "dev", None),
            P(None, "group", "dev", None),
            P("group", "dev", None),
            P(),
        ),
        out_specs=P(None, "group", "dev", None),
        check_vma=False,
    )
```

```python
import functools
import math

import jax
import jax.numpy as jnp
import numpy as np
from jax import lax
from jax.experimental import pallas as pl
from jax.experimental.pallas import tpu as pltpu
from jax.sharding import PartitionSpec as P

SWEEPS = 3
UNROLL = 4
LIMIT = 67043328
RELAX = 0.8
DAMPING = 0.5
MESH = pl.DeviceIdType.MESH

GROUPS, MEMBERS = 8, 16
DEVICES = GROUPS * MEMBERS
LX, LY, NZ = 64, 32, 256
CX, CY = LX // 4, LY // 4
PARTS = 4
PAD_X, PAD_Y = LX + 2, LY + 16
LANES = 128
TILES = LY // 8
F32 = jnp.float32


def block_real(matrix):
    return np.block([[matrix.real, -matrix.imag], [matrix.imag, matrix.real]])


def tables():
    count = 128
    z = np.arange(NZ) + 1
    basis = math.sqrt(2.0 / (NZ + 1)) * np.sin(math.pi / (NZ + 1) * np.outer(z, z))

    def dft(n):
        return np.exp(-2j * math.pi * np.outer(np.arange(n), np.arange(n)) / n)

    rows = np.kron(dft(GROUPS), dft(MEMBERS))
    lanes = np.kron(dft(CX), dft(CY))
    j1, k1 = np.repeat(np.arange(GROUPS), MEMBERS), np.tile(np.arange(MEMBERS), GROUPS)
    xi, yi = np.repeat(np.arange(CX), CY), np.tile(np.arange(CY), CX)
    twiddle = np.exp(-2j * math.pi * (np.outer(j1, xi) + np.outer(k1, yi)) / count)
    j2, k2 = xi, yi
    wave_x = j1[:, None] + GROUPS * j2[None, :]
    wave_y = k1[:, None] + MEMBERS * k2[None, :]
    eigen = (2 - 2 * np.cos(2 * math.pi * wave_x / count)) / 16
    eigen = eigen + (2 - 2 * np.cos(2 * math.pi * wave_y / count)) / 16
    vertical = 2 - 2 * np.cos(math.pi * z / (NZ + 1))
    forward_rows = block_real(rows)
    forward_lanes = block_real(lanes).T
    wide = [basis, forward_rows, forward_lanes, forward_lanes.T / count, forward_rows.T / count]
    narrow = [twiddle.real, twiddle.imag, eigen, np.tile(vertical[:, None], (1, LANES))]
    return np.float32(np.stack(wide)), np.float32(np.concatenate(narrow))


def dot(a, b, contract):
    def halved(value):
        high = value.astype(jnp.bfloat16)
        return high, (value - high.astype(F32)).astype(jnp.bfloat16)

    def product(u, v):
        return lax.dot_general(
            u, v, ((contract[:1], contract[1:]), ((), ())), preferred_element_type=F32)

    a_high, a_low = halved(a)
    b_high, b_low = halved(b)
    return product(a_high, b_high) + (product(a_high, b_low) + product(a_low, b_high))


def stencil(field, x, tile, absorb, lane):
    low = 8 + 8 * tile
    centre = [field[hc, x + 1, low : low + 8, :] for hc in range(4)]
    total = []
    for hc in range(4):
        beside = field[hc, x, low : low + 8, :] + field[hc, x + 2, low : low + 8, :]
        beside = beside + field[hc, x + 1, low - 1 : low + 7, :]
        beside = beside + field[hc, x + 1, low + 1 : low + 9, :]
        total.append(beside)
    after = [pltpu.roll(v, 1, axis=1) for v in centre]
    before = [pltpu.roll(v, LANES - 1, axis=1) for v in centre]
    robin = [
        centre[0] - absorb * centre[2],
        centre[1] - absorb * centre[3],
        centre[2] + absorb * centre[0],
        centre[3] + absorb * centre[1],
    ]
    first, final = lane == 0, lane == LANES - 1
    for c in range(2):
        a, b = 2 * c, 2 * c + 1
        total[a] = total[a] + jnp.where(first, robin[a], after[a])
        total[a] = total[a] + jnp.where(final, before[b], before[a])
        total[b] = total[b] + jnp.where(first, after[a], after[b])
        total[b] = total[b] + jnp.where(final, robin[b], before[b])
    return centre, total


def kernel(
    f_hbm, s_hbm, k_hbm, shift_ref, wide_hbm, narrow_hbm,
    out_hbm, edge_y_hbm, edge_x_hbm,
    fa, fb, res, edge_y, edge_x, src, wave, weight, absorb_ref, summed, coarse, wide, narrow,
    send1, recv1, send2, recv2,
    sy, sx, ry, rx, sey, sex, rey, rex,
    load_sem, part_sem, table_sem, a2a_sem, halo_send, halo_recv, store_sem, ready,
):
    g, d = lax.axis_index("group"), lax.axis_index("dev")
    me = g * MEMBERS + d

    barrier = pltpu.get_barrier_semaphore()

    column = [lax.rem(d + j, MEMBERS) for j in range(MEMBERS)]

    def everyone(start):
        order = [(2, 1), (1, 1), (3, 1), (2, 0), (0, 1), (1, 0), (3, 0), (0, 0)]
        columns = [
            4 * lax.rem(d // 4 + c, 4) + 2 * lax.rem(d // 2 + e, 2) + lax.rem(d + f, 2)
            for c, e in order for f in (1, 0)
        ]

        def row(i, carry):
            i = i + i // 5
            tg = 4 * lax.rem(g // 4 + 1 + i, 2) + lax.rem(g + 2 + 3 * (i // 2), 4)
            for td in columns:
                start(tg, td)
            return carry

        lax.fori_loop(0, GROUPS - 1, row, 0)
        for td in columns[:-1]:
            start(g, td)

    for ref in (ry, rx, rey, rex):
        ref[...] = jnp.zeros_like(ref)

    for i in range(1, GROUPS):
        pl.semaphore_signal(
            barrier, inc=1, device_id=(lax.rem(g + i, GROUPS), d), device_id_type=MESH)
    for td in column[1:]:
        pl.semaphore_signal(barrier, inc=1, device_id=(g, td), device_id_type=MESH)

    halves = [pl.ds(LANES * h, LANES) for h in range(2)]
    loads = []
    for hc in range(4):
        loads.append(pltpu.make_async_copy(
            f_hbm.at[hc // 2, :, :, halves[hc % 2]],
            fa.at[hc, pl.ds(1, LX), pl.ds(8, LY), :], load_sem.at[hc]))
    for copy in loads:
        copy.start()

    def part_loads(i):
        x = pl.ds(i * (LX // PARTS), LX // PARTS)
        copies = []
        for hc in range(4):
            copies.append(pltpu.make_async_copy(
                s_hbm.at[hc // 2, x, :, halves[hc % 2]], src.at[hc, x], part_sem.at[i, hc]))
        for h in range(2):
            copies.append(pltpu.make_async_copy(
                k_hbm.at[x, :, halves[h]], wave.at[h, x], part_sem.at[i, 4 + h]))
        return copies

    for i in range(PARTS):
        for copy in part_loads(i):
            copy.start()
    constants = [
        pltpu.make_async_copy(wide_hbm, wide, table_sem.at[0]),
        pltpu.make_async_copy(narrow_hbm, narrow, table_sem.at[1]),
    ]
    for copy in constants:
        copy.start()

    for ref in (fa, fb):
        ref[:, 0] = jnp.zeros((4, PAD_Y, LANES), F32)
        ref[:, PAD_X - 1] = jnp.zeros((4, PAD_Y, LANES), F32)

        def clear(x, carry, ref=ref):
            ref[:, x, 0:8, :] = jnp.zeros((4, 8, LANES), F32)
            ref[:, x, PAD_Y - 8 : PAD_Y, :] = jnp.zeros((4, 8, LANES), F32)
            return carry

        lax.fori_loop(1, PAD_X - 1, clear, 0)

    pl.semaphore_wait(barrier, GROUPS + MEMBERS - 2)
    for i in range(1, GROUPS):
        pl.semaphore_signal(
            ready, inc=1, device_id=(lax.rem(g + i, GROUPS), d), device_id_type=MESH)

    def sides(e, out_y, out_x, in_y, in_x):
        plan = []
        for side in range(2):
            step = 2 * side - 1
            for axis, (place, size, out, into) in enumerate(
                ((d, MEMBERS, out_y, in_y), (g, GROUPS, out_x, in_x))
            ):
                here = place > 0 if side == 0 else place < size - 1
                target = (g, d + step) if axis == 0 else (g + step, d)
                plan.append((
                    here,
                    pltpu.make_async_remote_copy(
                        src_ref=out.at[side], dst_ref=into.at[1 - side],
                        send_sem=halo_send.at[e, 2 * axis + side],
                        recv_sem=halo_recv.at[e, 2 * axis + 1 - side],
                        device_id=target, device_id_type=MESH),
                    pltpu.make_async_remote_copy(
                        src_ref=out.at[side], dst_ref=into.at[side],
                        send_sem=halo_send.at[e, 2 * axis + side],
                        recv_sem=halo_recv.at[e, 2 * axis + side],
                        device_id=target, device_id_type=MESH),
                ))
        return plan

    def start_sides(plan):
        for here, copy, _ in plan:
            pl.when(here)(copy.start)

    sent = []

    def finish_sides(plan):
        for here, _, arrived in plan:
            pl.when(here)(arrived.wait_recv)
            sent.append((here, arrived.wait_send))

    def pack(field, e):
        flat = field.reshape(4, PAD_X * PAD_Y, LANES)
        for hc in range(4):
            for side, row in ((0, 8), (1, 7 + LY)):
                sy[e, side, hc] = flat[hc, pl.ds(PAD_Y + row, LX, stride=PAD_Y), :]
            for side, x in ((0, 1), (1, LX)):
                sx[e, side, hc] = field[hc, x, 8 : 8 + LY, :]

    def beside(e):
        return sides(e, sy.at[e], sx.at[e], ry.at[e], rx.at[e])

    for copy in loads:
        copy.wait()
    pack(fa, 0)
    for hc in range(4):
        for side in range(2):
            sey[0, side, hc] = sum(
                sy[0, side, hc, pl.ds(q, CX, stride=4), :] for q in range(4))
            sex[0, side, hc] = sum(
                sx[0, side, hc, pl.ds(q, CY, stride=4), :] for q in range(4))
    sums = sides(4, sey.at[0], sex.at[0], rey.at[0], rex.at[0])
    start_sides(sums)
    start = beside(0)
    start_sides(start)

    lane = lax.broadcasted_iota(jnp.int32, (8, LANES), 1)
    sub = lax.broadcasted_iota(jnp.int32, (8, LANES), 0)

    def residual(xi, carry):
        for tile in range(TILES):
            rows = slice(8 * tile, 8 * tile + 8)
            sums = [None] * 4
            for q in range(4):
                x = 4 * xi + q
                k = [wave[h, x, rows, :] for h in range(2)]
                absorb = jnp.sqrt(jnp.where(lane < LANES // 2, k[0], k[1]))
                absorb_ref[x, rows, :] = absorb
                diagonal = [6.0 - v for v in k]
                for h in range(2):
                    weight[h, x, rows, :] = RELAX / diagonal[h]
                centre, total = stencil(fa, x, tile, absorb, lane)
                for hc in range(4):
                    value = src[hc, x, rows, :] + total[hc] - diagonal[hc % 2] * centre[hc]
                    sums[hc] = value if q == 0 else sums[hc] + value
            for hc in range(4):
                summed[hc, pl.ds(pl.multiple_of(xi * LY + 8 * tile, 8), 8), :] = sums[hc]
        return carry

    def residual_part(i, carry):
        for copy in part_loads(i):
            copy.wait()
        return lax.fori_loop(i * (CX // PARTS), (i + 1) * (CX // PARTS), residual, carry)

    lax.fori_loop(0, PARTS, residual_part, 0)
    for copy in constants:
        copy.wait()

    finish_sides(sums)
    cells = CX * CY
    for hc in range(4):
        value = summed[hc, pl.ds(0, cells, stride=4), :]
        for q in range(1, 4):
            value = value + summed[hc, pl.ds(q, cells, stride=4), :]
        coarse[hc] = value
        for side in range(2):
            at = pl.ds(7 * side, CX, stride=CY)
            coarse[hc, at, :] = coarse[hc, at, :] + rey[0, side, hc]
            at = pl.ds((CX - 1) * CY * side, CY)
            coarse[hc, at, :] = coarse[hc, at, :] + rex[0, side, hc]

    mean = jnp.concatenate(
        [jnp.concatenate([coarse[0], coarse[1]], axis=1),
         jnp.concatenate([coarse[2], coarse[3]], axis=1)], axis=0) * (1.0 / 16.0)
    modes = dot(wide[0], mean, (1, 1))
    send1_flat = send1.reshape(4 * DEVICES, LANES)
    for m in range(2):
        for c in range(2):
            send1_flat[pl.ds(2 * m + c, DEVICES, stride=4), :] = modes[
                DEVICES * m : DEVICES * (m + 1), LANES * c : LANES * (c + 1)]

    def to_all(source, target, index):

        def one(tg, td):
            pltpu.make_async_remote_copy(
                src_ref=source.at[tg * MEMBERS + td], dst_ref=target.at[me],
                send_sem=a2a_sem.at[2 * index], recv_sem=a2a_sem.at[2 * index + 1],
                device_id=(tg, td), device_id_type=MESH).start()

        everyone(one)
        target[me] = source[me]
        some = pl.ds(0, DEVICES - 1)
        sent.append((None, pltpu.make_async_copy(
            source.at[some], source.at[some], a2a_sem.at[2 * index]).wait))
        pltpu.make_async_copy(target.at[some], target.at[some], a2a_sem.at[2 * index + 1]).wait()

    pl.semaphore_wait(ready, GROUPS - 1)
    to_all(send1, recv1, 0)

    recv1_flat = recv1.reshape(4 * DEVICES, LANES)
    part = [recv1_flat[pl.ds(q, DEVICES, stride=4), :] for q in range(4)]
    planes = jnp.concatenate(
        [jnp.concatenate([part[0], part[2]], axis=1),
         jnp.concatenate([part[1], part[3]], axis=1)], axis=0)
    planes = dot(wide[1], planes, (1, 0))
    cosine, sine = narrow[0:LANES], narrow[LANES : 2 * LANES]

    def quarter(value, row, column):
        return value[LANES * row : LANES * (row + 1), LANES * column : LANES * (column + 1)]

    turned = []
    for m in range(2):
        real, imag = quarter(planes, 0, m), quarter(planes, 1, m)
        turned.append(jnp.concatenate(
            [real * cosine - imag * sine, real * sine + imag * cosine], axis=1))
    planes = dot(jnp.concatenate(turned, axis=0), wide[2], (1, 0))
    shift = shift_ref[0]
    imag_part = -DAMPING * shift
    solved = []
    for m in range(2):
        real, imag = quarter(planes, m, 0), quarter(planes, m, 1)
        height = narrow[pl.ds(3 * LANES + me + DEVICES * m, 1), :]
        real_part = narrow[2 * LANES : 3 * LANES] + (height - shift)
        modulus = real_part * real_part + imag_part * imag_part
        upper = (real * real_part + imag * imag_part) / modulus
        lower = (imag * real_part - real * imag_part) / modulus
        solved.append(jnp.concatenate([upper, lower], axis=1))
    planes = dot(jnp.concatenate(solved, axis=0), wide[3], (1, 0))
    turned = [[], []]
    for m in range(2):
        real, imag = quarter(planes, m, 0), quarter(planes, m, 1)
        turned[0].append(real * cosine + imag * sine)
        turned[1].append(imag * cosine - real * sine)
    planes = dot(
        wide[4],
        jnp.concatenate([jnp.concatenate(row, axis=1) for row in turned], axis=0), (1, 0))
    send2_flat = send2.reshape(4 * DEVICES, LANES)
    for m in range(2):
        for c in range(2):
            send2_flat[pl.ds(2 * m + c, DEVICES, stride=4), :] = quarter(planes, c, m)

    to_all(send2, recv2, 1)

    recv2_flat = recv2.reshape(4 * DEVICES, LANES)
    part = [recv2_flat[pl.ds(q, DEVICES, stride=4), :] for q in range(4)]
    modes = jnp.concatenate(
        [jnp.concatenate([part[0], part[1]], axis=1),
         jnp.concatenate([part[2], part[3]], axis=1)], axis=0)
    correction = dot(modes, wide[0], (0, 0))
    for c in range(2):
        for h in range(2):
            coarse[2 * c + h] = quarter(correction, c, h)

    for hc in range(4):
        for side in range(2):
            sey[1, side, hc] = coarse[hc, pl.ds(7 * side, CX, stride=CY), :]
            sex[1, side, hc] = coarse[hc, pl.ds((CX - 1) * CY * side, CY), :]
    edges = sides(3, sey.at[1], sex.at[1], rey.at[1], rex.at[1])
    start_sides(edges)

    def prolong(xi, carry):
        for tile in range(TILES):
            row = xi * CY + 2 * tile
            for hc in range(4):
                lower = jnp.broadcast_to(coarse[hc, pl.ds(row, 1), :], (8, LANES))
                upper = jnp.broadcast_to(coarse[hc, pl.ds(row + 1, 1), :], (8, LANES))
                spread = jnp.where(sub < 4, lower, upper)
                for q in range(4):
                    x = 4 * xi + q + 1
                    at = slice(8 + 8 * tile, 16 + 8 * tile)
                    fa[hc, x, at, :] = fa[hc, x, at, :] + spread
        return carry

    lax.fori_loop(0, CX, prolong, 0)

    def sweep(old, put, after=None):
        def some(i, carry):
            for tile in range(TILES):
                rows = slice(8 * tile, 8 * tile + 8)
                results = []
                for u in range(UNROLL):
                    x = UNROLL * i + u
                    centre, total = stencil(old, x, tile, absorb_ref[x, rows, :], lane)
                    for hc in range(4):
                        value = weight[hc % 2, x, rows, :] * (src[hc, x, rows, :] + total[hc])
                        results.append((hc, x, (1.0 - RELAX) * centre[hc] + value))
                for hc, x, value in results:
                    put(hc, x, tile, value)
            return carry

        steps = LX // UNROLL // PARTS

        def part(i, carry):
            lax.fori_loop(i * steps, (i + 1) * steps, some, carry)
            if after is not None:
                after(i)
            return carry

        lax.fori_loop(0, PARTS, part, 0)

    def into(field):
        def put(hc, x, tile, value):
            field[hc, x + 1, 8 + 8 * tile : 16 + 8 * tile, :] = value

        return put

    def put_out(hc, x, tile, value):
        res[hc // 2, x, 8 * tile : 8 * tile + 8, halves[hc % 2]] = value

    def stores(i):
        x = pl.ds(i * (LX // PARTS), LX // PARTS)
        return [pltpu.make_async_copy(res.at[c, x], out_hbm.at[c, x], store_sem.at[i, c])
                for c in range(2)]

    def start_stores(i):
        for copy in stores(i):
            copy.start()

    def add_halos(new, e):
        flat = new.reshape(4, PAD_X * PAD_Y, LANES)
        scale = weight.reshape(2, LX * LY, LANES)
        for hc in range(4):
            h = hc % 2
            for side, row in ((0, 0), (1, LY - 1)):
                at = pl.ds(PAD_Y + 8 + row, LX, stride=PAD_Y)
                flat[hc, at, :] = flat[hc, at, :] + (
                    scale[h, pl.ds(row, LX, stride=LY), :] * ry[e, side, hc])
            for side, x in ((0, 0), (1, LX - 1)):
                new[hc, x + 1, 8 : 8 + LY, :] = new[hc, x + 1, 8 : 8 + LY, :] + (
                    weight[h, x] * rx[e, side, hc])

    sweep(fa, into(fb))
    finish_sides(start)
    finish_sides(edges)
    for hc in range(4):
        for side in range(2):
            for q in range(4):
                at = pl.ds(q, CX, stride=4)
                ry[0, side, hc, at, :] = ry[0, side, hc, at, :] + rey[1, side, hc]
                at = pl.ds(q, CY, stride=4)
                rx[0, side, hc, at, :] = rx[0, side, hc, at, :] + rex[1, side, hc]
    add_halos(fb, 0)
    pack(fb, 1)
    plan = beside(1)
    start_sides(plan)
    sweep(fb, into(fa))
    finish_sides(plan)
    add_halos(fa, 1)
    pack(fa, 2)
    plan = beside(2)
    start_sides(plan)
    sweep(fa, put_out, start_stores)
    finish_sides(plan)
    scale = weight.reshape(2, LX * LY, LANES)
    for hc in range(4):
        h = hc % 2
        for side, row in ((0, 0), (1, LY - 1)):
            edge_y[side, hc] = scale[h, pl.ds(row, LX, stride=LY), :] * ry[2, side, hc]
        for side, x in ((0, 0), (1, LX - 1)):
            edge_x[side, hc] = weight[h, x] * rx[2, side, hc]
    last = [
        pltpu.make_async_copy(edge_y, edge_y_hbm, table_sem.at[0]),
        pltpu.make_async_copy(edge_x, edge_x_hbm, table_sem.at[1]),
    ]
    for copy in last:
        copy.start()
    for here, wait in sent:
        if here is None:
            wait()
        else:
            pl.when(here)(wait)
    for i in range(PARTS):
        for copy in stores(i):
            copy.wait()
    for copy in last:
        copy.wait()


def finish(parts, edge_y_hbm, edge_x_hbm, out_hbm, field, edge_y, edge_x, sem_in, sem_edge, sem_out):
    edges = [
        pltpu.make_async_copy(edge_y_hbm, edge_y, sem_edge.at[0]),
        pltpu.make_async_copy(edge_x_hbm, edge_x, sem_edge.at[1]),
    ]
    size = LX // PARTS
    halves = [slice(LANES * h, LANES * (h + 1)) for h in range(2)]
    blocks = [(c, i) for c in range(2) for i in range(PARTS)]

    def moves(source, target, sems):
        return [
            pltpu.make_async_copy(
                source.at[c, pl.ds(size * i, size)], target.at[c, pl.ds(size * i, size)],
                sems.at[c, i])
            for c, i in blocks
        ]

    loads = moves(parts, field, sem_in)
    stores = moves(field, out_hbm, sem_out)
    for copy in edges + loads:
        copy.start()
    for copy in edges:
        copy.wait()
    for (c, i), load, store in zip(blocks, loads, stores):
        load.wait()

        def rows(j, carry, c=c, i=i):
            for u in range(4):
                x = size * i + 4 * j + u
                for h in range(2):
                    for side, row in ((0, slice(0, 1)), (1, slice(LY - 1, LY))):
                        field[c, x, row, halves[h]] = field[c, x, row, halves[h]] + (
                            edge_y[side, 2 * c + h, pl.ds(x, 1), :])
            return carry

        lax.fori_loop(0, size // 4, rows, 0)
        for side, part in ((0, 0), (1, PARTS - 1)):
            if i == part:
                x = (LX - 1) * side
                for h in range(2):
                    field[c, x, :, halves[h]] = field[c, x, :, halves[h]] + (
                        edge_x[side, 2 * c + h])
        store.start()
    for store in stores:
        store.wait()


def body(field_now, source, wavenumber_sq, shift_sq):
    wide, narrow = tables()
    hbm = pl.BlockSpec(memory_space=pltpu.HBM)
    vmem = pltpu.VMEM
    dma = pltpu.SemaphoreType.DMA
    edges = [(2, 4, LX, LANES), (2, 4, LY, LANES)]
    parts = pl.pallas_call(
        kernel,
        out_shape=[jax.ShapeDtypeStruct(s, F32) for s in [field_now.shape] + edges],
        in_specs=[hbm] * 3 + [pl.BlockSpec(memory_space=pltpu.SMEM)] + [hbm] * 2,
        out_specs=[hbm] * 3,
        scratch_shapes=[
            vmem((4, PAD_X, PAD_Y, LANES), F32),
            vmem((4, PAD_X, PAD_Y, LANES), F32),
            vmem(field_now.shape, F32),
            vmem(edges[0], F32),
            vmem(edges[1], F32),
            vmem((4, LX, LY, LANES), F32),
            vmem((2, LX, LY, LANES), F32),
            vmem((2, LX, LY, LANES), F32),
            vmem((LX, LY, LANES), F32),
            vmem((4, CX * LY, LANES), F32),
            vmem((4, CX * CY, LANES), F32),
            vmem(wide.shape, F32),
            vmem(narrow.shape, F32),
        ] + [vmem((DEVICES, 4, LANES), F32)] * 4 + [
            vmem((3, 2, 4, LX, LANES), F32),
            vmem((3, 2, 4, LY, LANES), F32),
            vmem((3, 2, 4, LX, LANES), F32),
            vmem((3, 2, 4, LY, LANES), F32),
            vmem((2, 2, 4, CX, LANES), F32),
            vmem((2, 2, 4, CY, LANES), F32),
            vmem((2, 2, 4, CX, LANES), F32),
            vmem((2, 2, 4, CY, LANES), F32),
            dma((4,)),
            dma((PARTS, 6)),
            dma((2,)),
            dma((4,)),
            dma((5, 4)),
            dma((5, 4)),
            dma((PARTS, 2)),
            pltpu.SemaphoreType.REGULAR,
        ],
        compiler_params=pltpu.CompilerParams(
            collective_id=0, has_side_effects=True, vmem_limit_bytes=LIMIT),
        name="schwarz",
    )(field_now, source, wavenumber_sq, shift_sq, wide, narrow)
    return pl.pallas_call(
        finish,
        out_shape=jax.ShapeDtypeStruct(field_now.shape, F32),
        in_specs=[hbm] * 3,
        out_specs=hbm,
        scratch_shapes=[
            vmem(field_now.shape, F32),
            vmem(edges[0], F32),
            vmem(edges[1], F32),
            dma((2, PARTS)),
            dma((2,)),
            dma((2, PARTS)),
        ],
        compiler_params=pltpu.CompilerParams(vmem_limit_bytes=LIMIT),
        name="finish",
    )(*parts)


def solution(mesh):
    return jax.shard_map(
        body,
        mesh=mesh,
        in_specs=(
            P(None, "group", "dev", None),
            P(None, "group", "dev", None),
            P("group", "dev", None),
            P(),
        ),
        out_specs=P(None, "group", "dev", None),
        check_vma=False,
    )
```

```python
import functools
import math

import jax
import jax.numpy as jnp
import numpy as np
from jax import lax
from jax.experimental import pallas as pl
from jax.experimental.pallas import tpu as pltpu
from jax.sharding import PartitionSpec as P

SWEEPS = 3
UNROLL = 4
LIMIT = 67043328
RELAX = 0.8
DAMPING = 0.5
MESH = pl.DeviceIdType.MESH

GROUPS, MEMBERS = 8, 16
DEVICES = GROUPS * MEMBERS
LX, LY, NZ = 64, 32, 256
CX, CY = LX // 4, LY // 4
PARTS = 4
PAD_X, PAD_Y = LX + 2, LY + 16
LANES = 128
TILES = LY // 8
F32 = jnp.float32


def block_real(matrix):
    return np.block([[matrix.real, -matrix.imag], [matrix.imag, matrix.real]])


def tables():
    count = 128
    z = np.arange(NZ) + 1
    basis = math.sqrt(2.0 / (NZ + 1)) * np.sin(math.pi / (NZ + 1) * np.outer(z, z))

    def dft(n):
        return np.exp(-2j * math.pi * np.outer(np.arange(n), np.arange(n)) / n)

    rows = np.kron(dft(GROUPS), dft(MEMBERS))
    lanes = np.kron(dft(CX), dft(CY))
    j1, k1 = np.repeat(np.arange(GROUPS), MEMBERS), np.tile(np.arange(MEMBERS), GROUPS)
    xi, yi = np.repeat(np.arange(CX), CY), np.tile(np.arange(CY), CX)
    twiddle = np.exp(-2j * math.pi * (np.outer(j1, xi) + np.outer(k1, yi)) / count)
    j2, k2 = xi, yi
    wave_x = j1[:, None] + GROUPS * j2[None, :]
    wave_y = k1[:, None] + MEMBERS * k2[None, :]
    eigen = (2 - 2 * np.cos(2 * math.pi * wave_x / count)) / 16
    eigen = eigen + (2 - 2 * np.cos(2 * math.pi * wave_y / count)) / 16
    vertical = 2 - 2 * np.cos(math.pi * z / (NZ + 1))
    forward_rows = block_real(rows)
    forward_lanes = block_real(lanes).T
    wide = [basis, forward_rows, forward_lanes, forward_lanes.T / count, forward_rows.T / count]
    narrow = [twiddle.real, twiddle.imag, eigen, np.tile(vertical[:, None], (1, LANES))]
    return np.float32(np.stack(wide)), np.float32(np.concatenate(narrow))


def dot(a, b, contract):
    def halved(value):
        high = value.astype(jnp.bfloat16)
        return high, (value - high.astype(F32)).astype(jnp.bfloat16)

    def product(u, v):
        return lax.dot_general(
            u, v, ((contract[:1], contract[1:]), ((), ())), preferred_element_type=F32)

    a_high, a_low = halved(a)
    b_high, b_low = halved(b)
    return product(a_high, b_high) + (product(a_high, b_low) + product(a_low, b_high))


def stencil(field, x, tile, absorb, lane):
    low = 8 + 8 * tile
    centre = [field[hc, x + 1, low : low + 8, :] for hc in range(4)]
    total = []
    for hc in range(4):
        beside = field[hc, x, low : low + 8, :] + field[hc, x + 2, low : low + 8, :]
        beside = beside + field[hc, x + 1, low - 1 : low + 7, :]
        beside = beside + field[hc, x + 1, low + 1 : low + 9, :]
        total.append(beside)
    after = [pltpu.roll(v, 1, axis=1) for v in centre]
    before = [pltpu.roll(v, LANES - 1, axis=1) for v in centre]
    robin = [
        centre[0] - absorb * centre[2],
        centre[1] - absorb * centre[3],
        centre[2] + absorb * centre[0],
        centre[3] + absorb * centre[1],
    ]
    first, final = lane == 0, lane == LANES - 1
    for c in range(2):
        a, b = 2 * c, 2 * c + 1
        total[a] = total[a] + jnp.where(first, robin[a], after[a])
        total[a] = total[a] + jnp.where(final, before[b], before[a])
        total[b] = total[b] + jnp.where(first, after[a], after[b])
        total[b] = total[b] + jnp.where(final, robin[b], before[b])
    return centre, total


def kernel(
    f_hbm, s_hbm, k_hbm, shift_ref, wide_hbm, narrow_hbm,
    out_hbm, edge_y_hbm, edge_x_hbm,
    fa, fb, res, edge_y, edge_x, src, wave, weight, absorb_ref, summed, coarse, wide, narrow,
    send1, recv1, send2, recv2,
    sy, sx, ry, rx, sey, sex, rey, rex,
    load_sem, part_sem, table_sem, a2a_sem, halo_send, halo_recv, store_sem, ready,
):
    g, d = lax.axis_index("group"), lax.axis_index("dev")
    me = g * MEMBERS + d

    barrier = pltpu.get_barrier_semaphore()

    column = [lax.rem(d + j, MEMBERS) for j in range(MEMBERS)]

    def everyone(start):
        order = [(2, 1), (1, 1), (3, 1), (2, 0), (0, 1), (1, 0), (3, 0), (0, 0)]
        columns = [
            4 * lax.rem(d // 4 + c, 4) + 2 * lax.rem(d // 2 + e, 2) + lax.rem(d + f, 2)
            for c, e in order for f in (1, 0)
        ]

        def row(i, carry):
            i = i + i // 5
            tg = 4 * lax.rem(g // 4 + 1 + i, 2) + lax.rem(g + 2 + 3 * (i // 2), 4)
            for td in columns:
                start(tg, td)
            return carry

        lax.fori_loop(0, GROUPS - 1, row, 0)
        for td in columns[:-1]:
            start(g, td)

    for ref in (ry, rx, rey, rex):
        ref[...] = jnp.zeros_like(ref)

    for i in range(1, GROUPS):
        pl.semaphore_signal(
            barrier, inc=1, device_id=(lax.rem(g + i, GROUPS), d), device_id_type=MESH)
    for td in column[1:]:
        pl.semaphore_signal(barrier, inc=1, device_id=(g, td), device_id_type=MESH)

    halves = [pl.ds(LANES * h, LANES) for h in range(2)]
    loads = []
    for hc in range(4):
        loads.append(pltpu.make_async_copy(
            f_hbm.at[hc // 2, :, :, halves[hc % 2]],
            fa.at[hc, pl.ds(1, LX), pl.ds(8, LY), :], load_sem.at[hc]))
    for copy in loads:
        copy.start()

    def part_loads(i):
        x = pl.ds(i * (LX // PARTS), LX // PARTS)
        copies = []
        for hc in range(4):
            copies.append(pltpu.make_async_copy(
                s_hbm.at[hc // 2, x, :, halves[hc % 2]], src.at[hc, x], part_sem.at[i, hc]))
        for h in range(2):
            copies.append(pltpu.make_async_copy(
                k_hbm.at[x, :, halves[h]], wave.at[h, x], part_sem.at[i, 4 + h]))
        return copies

    for i in range(PARTS):
        for copy in part_loads(i):
            copy.start()
    constants = [
        pltpu.make_async_copy(wide_hbm, wide, table_sem.at[0]),
        pltpu.make_async_copy(narrow_hbm, narrow, table_sem.at[1]),
    ]
    for copy in constants:
        copy.start()

    for ref in (fa, fb):
        ref[:, 0] = jnp.zeros((4, PAD_Y, LANES), F32)
        ref[:, PAD_X - 1] = jnp.zeros((4, PAD_Y, LANES), F32)

        def clear(x, carry, ref=ref):
            ref[:, x, 0:8, :] = jnp.zeros((4, 8, LANES), F32)
            ref[:, x, PAD_Y - 8 : PAD_Y, :] = jnp.zeros((4, 8, LANES), F32)
            return carry

        lax.fori_loop(1, PAD_X - 1, clear, 0)

    pl.semaphore_wait(barrier, GROUPS + MEMBERS - 2)
    for i in range(1, GROUPS):
        pl.semaphore_signal(
            ready, inc=1, device_id=(lax.rem(g + i, GROUPS), d), device_id_type=MESH)

    def sides(e, out_y, out_x, in_y, in_x):
        plan = []
        for side in range(2):
            step = 2 * side - 1
            for axis, (place, size, out, into) in enumerate(
                ((d, MEMBERS, out_y, in_y), (g, GROUPS, out_x, in_x))
            ):
                here = place > 0 if side == 0 else place < size - 1
                target = (g, d + step) if axis == 0 else (g + step, d)
                plan.append((
                    here,
                    pltpu.make_async_remote_copy(
                        src_ref=out.at[side], dst_ref=into.at[1 - side],
                        send_sem=halo_send.at[e, 2 * axis + side],
                        recv_sem=halo_recv.at[e, 2 * axis + 1 - side],
                        device_id=target, device_id_type=MESH),
                    pltpu.make_async_remote_copy(
                        src_ref=out.at[side], dst_ref=into.at[side],
                        send_sem=halo_send.at[e, 2 * axis + side],
                        recv_sem=halo_recv.at[e, 2 * axis + side],
                        device_id=target, device_id_type=MESH),
                ))
        return plan

    def start_sides(plan):
        for here, copy, _ in plan:
            pl.when(here)(copy.start)

    sent = []

    def finish_sides(plan):
        for here, _, arrived in plan:
            pl.when(here)(arrived.wait_recv)
            sent.append((here, arrived.wait_send))

    def pack(field, e):
        flat = field.reshape(4, PAD_X * PAD_Y, LANES)
        for hc in range(4):
            for side, row in ((0, 8), (1, 7 + LY)):
                sy[e, side, hc] = flat[hc, pl.ds(PAD_Y + row, LX, stride=PAD_Y), :]
            for side, x in ((0, 1), (1, LX)):
                sx[e, side, hc] = field[hc, x, 8 : 8 + LY, :]

    def beside(e):
        return sides(e, sy.at[e], sx.at[e], ry.at[e], rx.at[e])

    for copy in loads:
        copy.wait()
    pack(fa, 0)
    for hc in range(4):
        for side in range(2):
            sey[0, side, hc] = sum(
                sy[0, side, hc, pl.ds(q, CX, stride=4), :] for q in range(4))
            sex[0, side, hc] = sum(
                sx[0, side, hc, pl.ds(q, CY, stride=4), :] for q in range(4))
    sums = sides(4, sey.at[0], sex.at[0], rey.at[0], rex.at[0])
    start_sides(sums)

    lane = lax.broadcasted_iota(jnp.int32, (8, LANES), 1)
    sub = lax.broadcasted_iota(jnp.int32, (8, LANES), 0)

    def residual(xi, carry):
        for tile in range(TILES):
            rows = slice(8 * tile, 8 * tile + 8)
            sums = [None] * 4
            for q in range(4):
                x = 4 * xi + q
                k = [wave[h, x, rows, :] for h in range(2)]
                absorb = jnp.sqrt(jnp.where(lane < LANES // 2, k[0], k[1]))
                absorb_ref[x, rows, :] = absorb
                diagonal = [6.0 - v for v in k]
                for h in range(2):
                    weight[h, x, rows, :] = RELAX / diagonal[h]
                centre, total = stencil(fa, x, tile, absorb, lane)
                for hc in range(4):
                    value = src[hc, x, rows, :] + total[hc] - diagonal[hc % 2] * centre[hc]
                    sums[hc] = value if q == 0 else sums[hc] + value
            for hc in range(4):
                summed[hc, pl.ds(pl.multiple_of(xi * LY + 8 * tile, 8), 8), :] = sums[hc]
        return carry

    def residual_part(i, carry):
        for copy in part_loads(i):
            copy.wait()
        return lax.fori_loop(i * (CX // PARTS), (i + 1) * (CX // PARTS), residual, carry)

    lax.fori_loop(0, PARTS, residual_part, 0)
    for copy in constants:
        copy.wait()

    finish_sides(sums)
    cells = CX * CY
    for hc in range(4):
        value = summed[hc, pl.ds(0, cells, stride=4), :]
        for q in range(1, 4):
            value = value + summed[hc, pl.ds(q, cells, stride=4), :]
        coarse[hc] = value
        for side in range(2):
            at = pl.ds(7 * side, CX, stride=CY)
            coarse[hc, at, :] = coarse[hc, at, :] + rey[0, side, hc]
            at = pl.ds((CX - 1) * CY * side, CY)
            coarse[hc, at, :] = coarse[hc, at, :] + rex[0, side, hc]

    mean = jnp.concatenate(
        [jnp.concatenate([coarse[0], coarse[1]], axis=1),
         jnp.concatenate([coarse[2], coarse[3]], axis=1)], axis=0) * (1.0 / 16.0)
    modes = dot(wide[0], mean, (1, 1))
    send1_flat = send1.reshape(4 * DEVICES, LANES)
    for m in range(2):
        for c in range(2):
            send1_flat[pl.ds(2 * m + c, DEVICES, stride=4), :] = modes[
                DEVICES * m : DEVICES * (m + 1), LANES * c : LANES * (c + 1)]

    def to_all(source, target, index):

        def one(tg, td):
            pltpu.make_async_remote_copy(
                src_ref=source.at[tg * MEMBERS + td], dst_ref=target.at[me],
                send_sem=a2a_sem.at[2 * index], recv_sem=a2a_sem.at[2 * index + 1],
                device_id=(tg, td), device_id_type=MESH).start()

        everyone(one)
        target[me] = source[me]
        some = pl.ds(0, DEVICES - 1)
        sent.append((None, pltpu.make_async_copy(
            source.at[some], source.at[some], a2a_sem.at[2 * index]).wait))
        pltpu.make_async_copy(target.at[some], target.at[some], a2a_sem.at[2 * index + 1]).wait()

    pl.semaphore_wait(ready, GROUPS - 1)
    to_all(send1, recv1, 0)
    start = beside(0)
    start_sides(start)

    recv1_flat = recv1.reshape(4 * DEVICES, LANES)
    part = [recv1_flat[pl.ds(q, DEVICES, stride=4), :] for q in range(4)]
    planes = jnp.concatenate(
        [jnp.concatenate([part[0], part[2]], axis=1),
         jnp.concatenate([part[1], part[3]], axis=1)], axis=0)
    planes = dot(wide[1], planes, (1, 0))
    cosine, sine = narrow[0:LANES], narrow[LANES : 2 * LANES]

    def quarter(value, row, column):
        return value[LANES * row : LANES * (row + 1), LANES * column : LANES * (column + 1)]

    turned = []
    for m in range(2):
        real, imag = quarter(planes, 0, m), quarter(planes, 1, m)
        turned.append(jnp.concatenate(
            [real * cosine - imag * sine, real * sine + imag * cosine], axis=1))
    planes = dot(jnp.concatenate(turned, axis=0), wide[2], (1, 0))
    shift = shift_ref[0]
    imag_part = -DAMPING * shift
    solved = []
    for m in range(2):
        real, imag = quarter(planes, m, 0), quarter(planes, m, 1)
        height = narrow[pl.ds(3 * LANES + me + DEVICES * m, 1), :]
        real_part = narrow[2 * LANES : 3 * LANES] + (height - shift)
        modulus = real_part * real_part + imag_part * imag_part
        upper = (real * real_part + imag * imag_part) / modulus
        lower = (imag * real_part - real * imag_part) / modulus
        solved.append(jnp.concatenate([upper, lower], axis=1))
    planes = dot(jnp.concatenate(solved, axis=0), wide[3], (1, 0))
    turned = [[], []]
    for m in range(2):
        real, imag = quarter(planes, m, 0), quarter(planes, m, 1)
        turned[0].append(real * cosine + imag * sine)
        turned[1].append(imag * cosine - real * sine)
    planes = dot(
        wide[4],
        jnp.concatenate([jnp.concatenate(row, axis=1) for row in turned], axis=0), (1, 0))
    send2_flat = send2.reshape(4 * DEVICES, LANES)
    for m in range(2):
        for c in range(2):
            send2_flat[pl.ds(2 * m + c, DEVICES, stride=4), :] = quarter(planes, c, m)

    to_all(send2, recv2, 1)

    recv2_flat = recv2.reshape(4 * DEVICES, LANES)
    part = [recv2_flat[pl.ds(q, DEVICES, stride=4), :] for q in range(4)]
    modes = jnp.concatenate(
        [jnp.concatenate([part[0], part[1]], axis=1),
         jnp.concatenate([part[2], part[3]], axis=1)], axis=0)
    correction = dot(modes, wide[0], (0, 0))
    for c in range(2):
        for h in range(2):
            coarse[2 * c + h] = quarter(correction, c, h)

    for hc in range(4):
        for side in range(2):
            sey[1, side, hc] = coarse[hc, pl.ds(7 * side, CX, stride=CY), :]
            sex[1, side, hc] = coarse[hc, pl.ds((CX - 1) * CY * side, CY), :]
    edges = sides(3, sey.at[1], sex.at[1], rey.at[1], rex.at[1])
    start_sides(edges)

    def prolong(xi, carry):
        for tile in range(TILES):
            row = xi * CY + 2 * tile
            for hc in range(4):
                lower = jnp.broadcast_to(coarse[hc, pl.ds(row, 1), :], (8, LANES))
                upper = jnp.broadcast_to(coarse[hc, pl.ds(row + 1, 1), :], (8, LANES))
                spread = jnp.where(sub < 4, lower, upper)
                for q in range(4):
                    x = 4 * xi + q + 1
                    at = slice(8 + 8 * tile, 16 + 8 * tile)
                    fa[hc, x, at, :] = fa[hc, x, at, :] + spread
        return carry

    lax.fori_loop(0, CX, prolong, 0)

    def sweep(old, put, after=None):
        def some(i, carry):
            for tile in range(TILES):
                rows = slice(8 * tile, 8 * tile + 8)
                results = []
                for u in range(UNROLL):
                    x = UNROLL * i + u
                    centre, total = stencil(old, x, tile, absorb_ref[x, rows, :], lane)
                    for hc in range(4):
                        value = weight[hc % 2, x, rows, :] * (src[hc, x, rows, :] + total[hc])
                        results.append((hc, x, (1.0 - RELAX) * centre[hc] + value))
                for hc, x, value in results:
                    put(hc, x, tile, value)
            return carry

        steps = LX // UNROLL // PARTS

        def part(i, carry):
            lax.fori_loop(i * steps, (i + 1) * steps, some, carry)
            if after is not None:
                after(i)
            return carry

        lax.fori_loop(0, PARTS, part, 0)

    def into(field):
        def put(hc, x, tile, value):
            field[hc, x + 1, 8 + 8 * tile : 16 + 8 * tile, :] = value

        return put

    def put_out(hc, x, tile, value):
        res[hc // 2, x, 8 * tile : 8 * tile + 8, halves[hc % 2]] = value

    def stores(i):
        x = pl.ds(i * (LX // PARTS), LX // PARTS)
        return [pltpu.make_async_copy(res.at[c, x], out_hbm.at[c, x], store_sem.at[i, c])
                for c in range(2)]

    def start_stores(i):
        for copy in stores(i):
            copy.start()

    def add_halos(new, e):
        flat = new.reshape(4, PAD_X * PAD_Y, LANES)
        scale = weight.reshape(2, LX * LY, LANES)
        for hc in range(4):
            h = hc % 2
            for side, row in ((0, 0), (1, LY - 1)):
                at = pl.ds(PAD_Y + 8 + row, LX, stride=PAD_Y)
                flat[hc, at, :] = flat[hc, at, :] + (
                    scale[h, pl.ds(row, LX, stride=LY), :] * ry[e, side, hc])
            for side, x in ((0, 0), (1, LX - 1)):
                new[hc, x + 1, 8 : 8 + LY, :] = new[hc, x + 1, 8 : 8 + LY, :] + (
                    weight[h, x] * rx[e, side, hc])

    sweep(fa, into(fb))
    finish_sides(start)
    finish_sides(edges)
    for hc in range(4):
        for side in range(2):
            for q in range(4):
                at = pl.ds(q, CX, stride=4)
                ry[0, side, hc, at, :] = ry[0, side, hc, at, :] + rey[1, side, hc]
                at = pl.ds(q, CY, stride=4)
                rx[0, side, hc, at, :] = rx[0, side, hc, at, :] + rex[1, side, hc]
    add_halos(fb, 0)
    pack(fb, 1)
    plan = beside(1)
    start_sides(plan)
    sweep(fb, into(fa))
    finish_sides(plan)
    add_halos(fa, 1)
    pack(fa, 2)
    plan = beside(2)
    start_sides(plan)
    sweep(fa, put_out, start_stores)
    finish_sides(plan)
    scale = weight.reshape(2, LX * LY, LANES)
    for hc in range(4):
        h = hc % 2
        for side, row in ((0, 0), (1, LY - 1)):
            edge_y[side, hc] = scale[h, pl.ds(row, LX, stride=LY), :] * ry[2, side, hc]
        for side, x in ((0, 0), (1, LX - 1)):
            edge_x[side, hc] = weight[h, x] * rx[2, side, hc]
    last = [
        pltpu.make_async_copy(edge_y, edge_y_hbm, table_sem.at[0]),
        pltpu.make_async_copy(edge_x, edge_x_hbm, table_sem.at[1]),
    ]
    for copy in last:
        copy.start()
    for here, wait in sent:
        if here is None:
            wait()
        else:
            pl.when(here)(wait)
    for i in range(PARTS):
        for copy in stores(i):
            copy.wait()
    for copy in last:
        copy.wait()


def finish(parts, edge_y_hbm, edge_x_hbm, out_hbm, field, edge_y, edge_x, sem_in, sem_edge, sem_out):
    edges = [
        pltpu.make_async_copy(edge_y_hbm, edge_y, sem_edge.at[0]),
        pltpu.make_async_copy(edge_x_hbm, edge_x, sem_edge.at[1]),
    ]
    size = LX // PARTS
    halves = [slice(LANES * h, LANES * (h + 1)) for h in range(2)]
    blocks = [(c, i) for c in range(2) for i in range(PARTS)]

    def moves(source, target, sems):
        return [
            pltpu.make_async_copy(
                source.at[c, pl.ds(size * i, size)], target.at[c, pl.ds(size * i, size)],
                sems.at[c, i])
            for c, i in blocks
        ]

    loads = moves(parts, field, sem_in)
    stores = moves(field, out_hbm, sem_out)
    for copy in edges + loads:
        copy.start()
    for copy in edges:
        copy.wait()
    for (c, i), load, store in zip(blocks, loads, stores):
        load.wait()

        def rows(j, carry, c=c, i=i):
            for u in range(4):
                x = size * i + 4 * j + u
                for h in range(2):
                    for side, row in ((0, slice(0, 1)), (1, slice(LY - 1, LY))):
                        field[c, x, row, halves[h]] = field[c, x, row, halves[h]] + (
                            edge_y[side, 2 * c + h, pl.ds(x, 1), :])
            return carry

        lax.fori_loop(0, size // 4, rows, 0)
        for side, part in ((0, 0), (1, PARTS - 1)):
            if i == part:
                x = (LX - 1) * side
                for h in range(2):
                    field[c, x, :, halves[h]] = field[c, x, :, halves[h]] + (
                        edge_x[side, 2 * c + h])
        store.start()
    for store in stores:
        store.wait()


def body(field_now, source, wavenumber_sq, shift_sq):
    wide, narrow = tables()
    hbm = pl.BlockSpec(memory_space=pltpu.HBM)
    vmem = pltpu.VMEM
    dma = pltpu.SemaphoreType.DMA
    edges = [(2, 4, LX, LANES), (2, 4, LY, LANES)]
    parts = pl.pallas_call(
        kernel,
        out_shape=[jax.ShapeDtypeStruct(s, F32) for s in [field_now.shape] + edges],
        in_specs=[hbm] * 3 + [pl.BlockSpec(memory_space=pltpu.SMEM)] + [hbm] * 2,
        out_specs=[hbm] * 3,
        scratch_shapes=[
            vmem((4, PAD_X, PAD_Y, LANES), F32),
            vmem((4, PAD_X, PAD_Y, LANES), F32),
            vmem(field_now.shape, F32),
            vmem(edges[0], F32),
            vmem(edges[1], F32),
            vmem((4, LX, LY, LANES), F32),
            vmem((2, LX, LY, LANES), F32),
            vmem((2, LX, LY, LANES), F32),
            vmem((LX, LY, LANES), F32),
            vmem((4, CX * LY, LANES), F32),
            vmem((4, CX * CY, LANES), F32),
            vmem(wide.shape, F32),
            vmem(narrow.shape, F32),
        ] + [vmem((DEVICES, 4, LANES), F32)] * 4 + [
            vmem((3, 2, 4, LX, LANES), F32),
            vmem((3, 2, 4, LY, LANES), F32),
            vmem((3, 2, 4, LX, LANES), F32),
            vmem((3, 2, 4, LY, LANES), F32),
            vmem((2, 2, 4, CX, LANES), F32),
            vmem((2, 2, 4, CY, LANES), F32),
            vmem((2, 2, 4, CX, LANES), F32),
            vmem((2, 2, 4, CY, LANES), F32),
            dma((4,)),
            dma((PARTS, 6)),
            dma((2,)),
            dma((4,)),
            dma((5, 4)),
            dma((5, 4)),
            dma((PARTS, 2)),
            pltpu.SemaphoreType.REGULAR,
        ],
        compiler_params=pltpu.CompilerParams(
            collective_id=0, has_side_effects=True, vmem_limit_bytes=LIMIT),
        name="schwarz",
    )(field_now, source, wavenumber_sq, shift_sq, wide, narrow)
    return pl.pallas_call(
        finish,
        out_shape=jax.ShapeDtypeStruct(field_now.shape, F32),
        in_specs=[hbm] * 3,
        out_specs=hbm,
        scratch_shapes=[
            vmem(field_now.shape, F32),
            vmem(edges[0], F32),
            vmem(edges[1], F32),
            dma((2, PARTS)),
            dma((2,)),
            dma((2, PARTS)),
        ],
        compiler_params=pltpu.CompilerParams(vmem_limit_bytes=LIMIT),
        name="finish",
    )(*parts)


def solution(mesh):
    return jax.shard_map(
        body,
        mesh=mesh,
        in_specs=(
            P(None, "group", "dev", None),
            P(None, "group", "dev", None),
            P("group", "dev", None),
            P(),
        ),
        out_specs=P(None, "group", "dev", None),
        check_vma=False,
    )
```

```python
import functools
import math

import jax
import jax.numpy as jnp
import numpy as np
from jax import lax
from jax.experimental import pallas as pl
from jax.experimental.pallas import tpu as pltpu
from jax.sharding import PartitionSpec as P

SWEEPS = 3
UNROLL = 4
LIMIT = 67043328
RELAX = 0.8
DAMPING = 0.5
MESH = pl.DeviceIdType.MESH

GROUPS, MEMBERS = 8, 16
DEVICES = GROUPS * MEMBERS
LX, LY, NZ = 64, 32, 256
CX, CY = LX // 4, LY // 4
PARTS = 8
PAD_X, PAD_Y = LX + 2, LY + 16
LANES = 128
TILES = LY // 8
F32 = jnp.float32


def block_real(matrix):
    return np.block([[matrix.real, -matrix.imag], [matrix.imag, matrix.real]])


def tables():
    count = 128
    z = np.arange(NZ) + 1
    basis = math.sqrt(2.0 / (NZ + 1)) * np.sin(math.pi / (NZ + 1) * np.outer(z, z))

    def dft(n):
        return np.exp(-2j * math.pi * np.outer(np.arange(n), np.arange(n)) / n)

    rows = np.kron(dft(GROUPS), dft(MEMBERS))
    lanes = np.kron(dft(CX), dft(CY))
    j1, k1 = np.repeat(np.arange(GROUPS), MEMBERS), np.tile(np.arange(MEMBERS), GROUPS)
    xi, yi = np.repeat(np.arange(CX), CY), np.tile(np.arange(CY), CX)
    twiddle = np.exp(-2j * math.pi * (np.outer(j1, xi) + np.outer(k1, yi)) / count)
    j2, k2 = xi, yi
    wave_x = j1[:, None] + GROUPS * j2[None, :]
    wave_y = k1[:, None] + MEMBERS * k2[None, :]
    eigen = (2 - 2 * np.cos(2 * math.pi * wave_x / count)) / 16
    eigen = eigen + (2 - 2 * np.cos(2 * math.pi * wave_y / count)) / 16
    vertical = 2 - 2 * np.cos(math.pi * z / (NZ + 1))
    forward_rows = block_real(rows)
    forward_lanes = block_real(lanes).T
    wide = [basis, forward_rows, forward_lanes, forward_lanes.T / count, forward_rows.T / count]
    narrow = [twiddle.real, twiddle.imag, eigen, np.tile(vertical[:, None], (1, LANES))]
    return np.float32(np.stack(wide)), np.float32(np.concatenate(narrow))


def dot(a, b, contract):
    def halved(value):
        high = value.astype(jnp.bfloat16)
        return high, (value - high.astype(F32)).astype(jnp.bfloat16)

    def product(u, v):
        return lax.dot_general(
            u, v, ((contract[:1], contract[1:]), ((), ())), preferred_element_type=F32)

    a_high, a_low = halved(a)
    b_high, b_low = halved(b)
    return product(a_high, b_high) + (product(a_high, b_low) + product(a_low, b_high))


def stencil(field, x, tile, absorb, lane):
    low = 8 + 8 * tile
    centre = [field[hc, x + 1, low : low + 8, :] for hc in range(4)]
    total = []
    for hc in range(4):
        beside = field[hc, x, low : low + 8, :] + field[hc, x + 2, low : low + 8, :]
        beside = beside + field[hc, x + 1, low - 1 : low + 7, :]
        beside = beside + field[hc, x + 1, low + 1 : low + 9, :]
        total.append(beside)
    after = [pltpu.roll(v, 1, axis=1) for v in centre]
    before = [pltpu.roll(v, LANES - 1, axis=1) for v in centre]
    robin = [
        centre[0] - absorb * centre[2],
        centre[1] - absorb * centre[3],
        centre[2] + absorb * centre[0],
        centre[3] + absorb * centre[1],
    ]
    first, final = lane == 0, lane == LANES - 1
    for c in range(2):
        a, b = 2 * c, 2 * c + 1
        total[a] = total[a] + jnp.where(first, robin[a], after[a])
        total[a] = total[a] + jnp.where(final, before[b], before[a])
        total[b] = total[b] + jnp.where(first, after[a], after[b])
        total[b] = total[b] + jnp.where(final, robin[b], before[b])
    return centre, total


def kernel(
    f_hbm, s_hbm, k_hbm, shift_ref, wide_hbm, narrow_hbm,
    out_hbm, edge_y_hbm, edge_x_hbm,
    fa, fb, res, edge_y, edge_x, src, wave, weight, absorb_ref, summed, coarse, wide, narrow,
    send1, recv1, send2, recv2,
    sy, sx, ry, rx, sey, sex, rey, rex,
    load_sem, part_sem, table_sem, a2a_sem, halo_send, halo_recv, store_sem, ready,
):
    g, d = lax.axis_index("group"), lax.axis_index("dev")
    me = g * MEMBERS + d

    barrier = pltpu.get_barrier_semaphore()

    column = [lax.rem(d + j, MEMBERS) for j in range(MEMBERS)]

    def everyone(start):
        order = [(2, 1), (1, 1), (3, 1), (2, 0), (0, 1), (1, 0), (3, 0), (0, 0)]
        columns = [
            4 * lax.rem(d // 4 + c, 4) + 2 * lax.rem(d // 2 + e, 2) + lax.rem(d + f, 2)
            for c, e in order for f in (1, 0)
        ]

        def row(i, carry):
            i = i + i // 5
            tg = 4 * lax.rem(g // 4 + 1 + i, 2) + lax.rem(g + 2 + 3 * (i // 2), 4)
            for td in columns:
                start(tg, td)
            return carry

        lax.fori_loop(0, GROUPS - 1, row, 0)
        for td in columns[:-1]:
            start(g, td)

    for ref in (ry, rx, rey, rex):
        ref[...] = jnp.zeros_like(ref)

    for i in range(1, GROUPS):
        pl.semaphore_signal(
            barrier, inc=1, device_id=(lax.rem(g + i, GROUPS), d), device_id_type=MESH)
    for td in column[1:]:
        pl.semaphore_signal(barrier, inc=1, device_id=(g, td), device_id_type=MESH)

    halves = [pl.ds(LANES * h, LANES) for h in range(2)]
    loads = []
    for hc in range(4):
        loads.append(pltpu.make_async_copy(
            f_hbm.at[hc // 2, :, :, halves[hc % 2]],
            fa.at[hc, pl.ds(1, LX), pl.ds(8, LY), :], load_sem.at[hc]))
    for copy in loads:
        copy.start()

    def part_loads(i):
        x = pl.ds(i * (LX // PARTS), LX // PARTS)
        copies = []
        for hc in range(4):
            copies.append(pltpu.make_async_copy(
                s_hbm.at[hc // 2, x, :, halves[hc % 2]], src.at[hc, x], part_sem.at[i, hc]))
        for h in range(2):
            copies.append(pltpu.make_async_copy(
                k_hbm.at[x, :, halves[h]], wave.at[h, x], part_sem.at[i, 4 + h]))
        return copies

    for i in range(PARTS):
        for copy in part_loads(i):
            copy.start()
    constants = [
        pltpu.make_async_copy(wide_hbm, wide, table_sem.at[0]),
        pltpu.make_async_copy(narrow_hbm, narrow, table_sem.at[1]),
    ]
    for copy in constants:
        copy.start()

    for ref in (fa, fb):
        ref[:, 0] = jnp.zeros((4, PAD_Y, LANES), F32)
        ref[:, PAD_X - 1] = jnp.zeros((4, PAD_Y, LANES), F32)

        def clear(x, carry, ref=ref):
            ref[:, x, 0:8, :] = jnp.zeros((4, 8, LANES), F32)
            ref[:, x, PAD_Y - 8 : PAD_Y, :] = jnp.zeros((4, 8, LANES), F32)
            return carry

        lax.fori_loop(1, PAD_X - 1, clear, 0)

    pl.semaphore_wait(barrier, GROUPS + MEMBERS - 2)
    for i in range(1, GROUPS):
        pl.semaphore_signal(
            ready, inc=1, device_id=(lax.rem(g + i, GROUPS), d), device_id_type=MESH)

    def sides(e, out_y, out_x, in_y, in_x):
        plan = []
        for side in range(2):
            step = 2 * side - 1
            for axis, (place, size, out, into) in enumerate(
                ((d, MEMBERS, out_y, in_y), (g, GROUPS, out_x, in_x))
            ):
                here = place > 0 if side == 0 else place < size - 1
                target = (g, d + step) if axis == 0 else (g + step, d)
                plan.append((
                    here,
                    pltpu.make_async_remote_copy(
                        src_ref=out.at[side], dst_ref=into.at[1 - side],
                        send_sem=halo_send.at[e, 2 * axis + side],
                        recv_sem=halo_recv.at[e, 2 * axis + 1 - side],
                        device_id=target, device_id_type=MESH),
                    pltpu.make_async_remote_copy(
                        src_ref=out.at[side], dst_ref=into.at[side],
                        send_sem=halo_send.at[e, 2 * axis + side],
                        recv_sem=halo_recv.at[e, 2 * axis + side],
                        device_id=target, device_id_type=MESH),
                ))
        return plan

    def start_sides(plan):
        for here, copy, _ in plan:
            pl.when(here)(copy.start)

    sent = []

    def finish_sides(plan):
        for here, _, arrived in plan:
            pl.when(here)(arrived.wait_recv)
            sent.append((here, arrived.wait_send))

    def pack(field, e):
        flat = field.reshape(4, PAD_X * PAD_Y, LANES)
        for hc in range(4):
            for side, row in ((0, 8), (1, 7 + LY)):
                sy[e, side, hc] = flat[hc, pl.ds(PAD_Y + row, LX, stride=PAD_Y), :]
            for side, x in ((0, 1), (1, LX)):
                sx[e, side, hc] = field[hc, x, 8 : 8 + LY, :]

    def beside(e):
        return sides(e, sy.at[e], sx.at[e], ry.at[e], rx.at[e])

    for copy in loads:
        copy.wait()
    pack(fa, 0)
    for hc in range(4):
        for side in range(2):
            sey[0, side, hc] = sum(
                sy[0, side, hc, pl.ds(q, CX, stride=4), :] for q in range(4))
            sex[0, side, hc] = sum(
                sx[0, side, hc, pl.ds(q, CY, stride=4), :] for q in range(4))
    sums = sides(4, sey.at[0], sex.at[0], rey.at[0], rex.at[0])
    start_sides(sums)

    lane = lax.broadcasted_iota(jnp.int32, (8, LANES), 1)
    sub = lax.broadcasted_iota(jnp.int32, (8, LANES), 0)

    def residual(xi, carry):
        for tile in range(TILES):
            rows = slice(8 * tile, 8 * tile + 8)
            sums = [None] * 4
            for q in range(4):
                x = 4 * xi + q
                k = [wave[h, x, rows, :] for h in range(2)]
                absorb = jnp.sqrt(jnp.where(lane < LANES // 2, k[0], k[1]))
                absorb_ref[x, rows, :] = absorb
                diagonal = [6.0 - v for v in k]
                for h in range(2):
                    weight[h, x, rows, :] = RELAX / diagonal[h]
                centre, total = stencil(fa, x, tile, absorb, lane)
                for hc in range(4):
                    value = src[hc, x, rows, :] + total[hc] - diagonal[hc % 2] * centre[hc]
                    sums[hc] = value if q == 0 else sums[hc] + value
            for hc in range(4):
                summed[hc, pl.ds(pl.multiple_of(xi * LY + 8 * tile, 8), 8), :] = sums[hc]
        return carry

    def residual_part(i, carry):
        for copy in part_loads(i):
            copy.wait()
        return lax.fori_loop(i * (CX // PARTS), (i + 1) * (CX // PARTS), residual, carry)

    lax.fori_loop(0, PARTS, residual_part, 0)
    for copy in constants:
        copy.wait()

    finish_sides(sums)
    cells = CX * CY
    for hc in range(4):
        value = summed[hc, pl.ds(0, cells, stride=4), :]
        for q in range(1, 4):
            value = value + summed[hc, pl.ds(q, cells, stride=4), :]
        coarse[hc] = value
        for side in range(2):
            at = pl.ds(7 * side, CX, stride=CY)
            coarse[hc, at, :] = coarse[hc, at, :] + rey[0, side, hc]
            at = pl.ds((CX - 1) * CY * side, CY)
            coarse[hc, at, :] = coarse[hc, at, :] + rex[0, side, hc]

    mean = jnp.concatenate(
        [jnp.concatenate([coarse[0], coarse[1]], axis=1),
         jnp.concatenate([coarse[2], coarse[3]], axis=1)], axis=0) * (1.0 / 16.0)
    modes = dot(wide[0], mean, (1, 1))
    send1_flat = send1.reshape(4 * DEVICES, LANES)
    for m in range(2):
        for c in range(2):
            send1_flat[pl.ds(2 * m + c, DEVICES, stride=4), :] = modes[
                DEVICES * m : DEVICES * (m + 1), LANES * c : LANES * (c + 1)]

    def to_all(source, target, index):

        def one(tg, td):
            pltpu.make_async_remote_copy(
                src_ref=source.at[tg * MEMBERS + td], dst_ref=target.at[me],
                send_sem=a2a_sem.at[2 * index], recv_sem=a2a_sem.at[2 * index + 1],
                device_id=(tg, td), device_id_type=MESH).start()

        everyone(one)
        target[me] = source[me]
        some = pl.ds(0, DEVICES - 1)
        sent.append((None, pltpu.make_async_copy(
            source.at[some], source.at[some], a2a_sem.at[2 * index]).wait))
        pltpu.make_async_copy(target.at[some], target.at[some], a2a_sem.at[2 * index + 1]).wait()

    pl.semaphore_wait(ready, GROUPS - 1)
    to_all(send1, recv1, 0)
    start = beside(0)
    start_sides(start)

    recv1_flat = recv1.reshape(4 * DEVICES, LANES)
    part = [recv1_flat[pl.ds(q, DEVICES, stride=4), :] for q in range(4)]
    planes = jnp.concatenate(
        [jnp.concatenate([part[0], part[2]], axis=1),
         jnp.concatenate([part[1], part[3]], axis=1)], axis=0)
    planes = dot(wide[1], planes, (1, 0))
    cosine, sine = narrow[0:LANES], narrow[LANES : 2 * LANES]

    def quarter(value, row, column):
        return value[LANES * row : LANES * (row + 1), LANES * column : LANES * (column + 1)]

    turned = []
    for m in range(2):
        real, imag = quarter(planes, 0, m), quarter(planes, 1, m)
        turned.append(jnp.concatenate(
            [real * cosine - imag * sine, real * sine + imag * cosine], axis=1))
    planes = dot(jnp.concatenate(turned, axis=0), wide[2], (1, 0))
    shift = shift_ref[0]
    imag_part = -DAMPING * shift
    solved = []
    for m in range(2):
        real, imag = quarter(planes, m, 0), quarter(planes, m, 1)
        height = narrow[pl.ds(3 * LANES + me + DEVICES * m, 1), :]
        real_part = narrow[2 * LANES : 3 * LANES] + (height - shift)
        modulus = real_part * real_part + imag_part * imag_part
        upper = (real * real_part + imag * imag_part) / modulus
        lower = (imag * real_part - real * imag_part) / modulus
        solved.append(jnp.concatenate([upper, lower], axis=1))
    planes = dot(jnp.concatenate(solved, axis=0), wide[3], (1, 0))
    turned = [[], []]
    for m in range(2):
        real, imag = quarter(planes, m, 0), quarter(planes, m, 1)
        turned[0].append(real * cosine + imag * sine)
        turned[1].append(imag * cosine - real * sine)
    planes = dot(
        wide[4],
        jnp.concatenate([jnp.concatenate(row, axis=1) for row in turned], axis=0), (1, 0))
    send2_flat = send2.reshape(4 * DEVICES, LANES)
    for m in range(2):
        for c in range(2):
            send2_flat[pl.ds(2 * m + c, DEVICES, stride=4), :] = quarter(planes, c, m)

    to_all(send2, recv2, 1)

    recv2_flat = recv2.reshape(4 * DEVICES, LANES)
    part = [recv2_flat[pl.ds(q, DEVICES, stride=4), :] for q in range(4)]
    modes = jnp.concatenate(
        [jnp.concatenate([part[0], part[1]], axis=1),
         jnp.concatenate([part[2], part[3]], axis=1)], axis=0)
    correction = dot(modes, wide[0], (0, 0))
    for c in range(2):
        for h in range(2):
            coarse[2 * c + h] = quarter(correction, c, h)

    for hc in range(4):
        for side in range(2):
            sey[1, side, hc] = coarse[hc, pl.ds(7 * side, CX, stride=CY), :]
            sex[1, side, hc] = coarse[hc, pl.ds((CX - 1) * CY * side, CY), :]
    edges = sides(3, sey.at[1], sex.at[1], rey.at[1], rex.at[1])
    start_sides(edges)

    def prolong(xi, carry):
        for tile in range(TILES):
            row = xi * CY + 2 * tile
            for hc in range(4):
                lower = jnp.broadcast_to(coarse[hc, pl.ds(row, 1), :], (8, LANES))
                upper = jnp.broadcast_to(coarse[hc, pl.ds(row + 1, 1), :], (8, LANES))
                spread = jnp.where(sub < 4, lower, upper)
                for q in range(4):
                    x = 4 * xi + q + 1
                    at = slice(8 + 8 * tile, 16 + 8 * tile)
                    fa[hc, x, at, :] = fa[hc, x, at, :] + spread
        return carry

    lax.fori_loop(0, CX, prolong, 0)

    def sweep(old, put, after=None):
        def some(i, carry):
            for tile in range(TILES):
                rows = slice(8 * tile, 8 * tile + 8)
                results = []
                for u in range(UNROLL):
                    x = UNROLL * i + u
                    centre, total = stencil(old, x, tile, absorb_ref[x, rows, :], lane)
                    for hc in range(4):
                        value = weight[hc % 2, x, rows, :] * (src[hc, x, rows, :] + total[hc])
                        results.append((hc, x, (1.0 - RELAX) * centre[hc] + value))
                for hc, x, value in results:
                    put(hc, x, tile, value)
            return carry

        steps = LX // UNROLL // PARTS

        def part(i, carry):
            lax.fori_loop(i * steps, (i + 1) * steps, some, carry)
            if after is not None:
                after(i)
            return carry

        lax.fori_loop(0, PARTS, part, 0)

    def into(field):
        def put(hc, x, tile, value):
            field[hc, x + 1, 8 + 8 * tile : 16 + 8 * tile, :] = value

        return put

    def put_out(hc, x, tile, value):
        res[hc // 2, x, 8 * tile : 8 * tile + 8, halves[hc % 2]] = value

    def stores(i):
        x = pl.ds(i * (LX // PARTS), LX // PARTS)
        return [pltpu.make_async_copy(res.at[c, x], out_hbm.at[c, x], store_sem.at[i, c])
                for c in range(2)]

    def start_stores(i):
        for copy in stores(i):
            copy.start()

    def add_halos(new, e):
        flat = new.reshape(4, PAD_X * PAD_Y, LANES)
        scale = weight.reshape(2, LX * LY, LANES)
        for hc in range(4):
            h = hc % 2
            for side, row in ((0, 0), (1, LY - 1)):
                at = pl.ds(PAD_Y + 8 + row, LX, stride=PAD_Y)
                flat[hc, at, :] = flat[hc, at, :] + (
                    scale[h, pl.ds(row, LX, stride=LY), :] * ry[e, side, hc])
            for side, x in ((0, 0), (1, LX - 1)):
                new[hc, x + 1, 8 : 8 + LY, :] = new[hc, x + 1, 8 : 8 + LY, :] + (
                    weight[h, x] * rx[e, side, hc])

    sweep(fa, into(fb))
    finish_sides(start)
    finish_sides(edges)
    for hc in range(4):
        for side in range(2):
            for q in range(4):
                at = pl.ds(q, CX, stride=4)
                ry[0, side, hc, at, :] = ry[0, side, hc, at, :] + rey[1, side, hc]
                at = pl.ds(q, CY, stride=4)
                rx[0, side, hc, at, :] = rx[0, side, hc, at, :] + rex[1, side, hc]
    add_halos(fb, 0)
    pack(fb, 1)
    plan = beside(1)
    start_sides(plan)
    sweep(fb, into(fa))
    finish_sides(plan)
    add_halos(fa, 1)
    pack(fa, 2)
    plan = beside(2)
    start_sides(plan)
    sweep(fa, put_out, start_stores)
    finish_sides(plan)
    scale = weight.reshape(2, LX * LY, LANES)
    for hc in range(4):
        h = hc % 2
        for side, row in ((0, 0), (1, LY - 1)):
            edge_y[side, hc] = scale[h, pl.ds(row, LX, stride=LY), :] * ry[2, side, hc]
        for side, x in ((0, 0), (1, LX - 1)):
            edge_x[side, hc] = weight[h, x] * rx[2, side, hc]
    last = [
        pltpu.make_async_copy(edge_y, edge_y_hbm, table_sem.at[0]),
        pltpu.make_async_copy(edge_x, edge_x_hbm, table_sem.at[1]),
    ]
    for copy in last:
        copy.start()
    for here, wait in sent:
        if here is None:
            wait()
        else:
            pl.when(here)(wait)
    for i in range(PARTS):
        for copy in stores(i):
            copy.wait()
    for copy in last:
        copy.wait()


def finish(parts, edge_y_hbm, edge_x_hbm, out_hbm, field, edge_y, edge_x, sem_in, sem_edge, sem_out):
    edges = [
        pltpu.make_async_copy(edge_y_hbm, edge_y, sem_edge.at[0]),
        pltpu.make_async_copy(edge_x_hbm, edge_x, sem_edge.at[1]),
    ]
    size = LX // PARTS
    halves = [slice(LANES * h, LANES * (h + 1)) for h in range(2)]
    blocks = [(c, i) for c in range(2) for i in range(PARTS)]

    def moves(source, target, sems):
        return [
            pltpu.make_async_copy(
                source.at[c, pl.ds(size * i, size)], target.at[c, pl.ds(size * i, size)],
                sems.at[c, i])
            for c, i in blocks
        ]

    loads = moves(parts, field, sem_in)
    stores = moves(field, out_hbm, sem_out)
    for copy in edges + loads:
        copy.start()
    for copy in edges:
        copy.wait()
    for (c, i), load, store in zip(blocks, loads, stores):
        load.wait()

        def rows(j, carry, c=c, i=i):
            for u in range(4):
                x = size * i + 4 * j + u
                for h in range(2):
                    for side, row in ((0, slice(0, 1)), (1, slice(LY - 1, LY))):
                        field[c, x, row, halves[h]] = field[c, x, row, halves[h]] + (
                            edge_y[side, 2 * c + h, pl.ds(x, 1), :])
            return carry

        lax.fori_loop(0, size // 4, rows, 0)
        for side, part in ((0, 0), (1, PARTS - 1)):
            if i == part:
                x = (LX - 1) * side
                for h in range(2):
                    field[c, x, :, halves[h]] = field[c, x, :, halves[h]] + (
                        edge_x[side, 2 * c + h])
        store.start()
    for store in stores:
        store.wait()


def body(field_now, source, wavenumber_sq, shift_sq):
    wide, narrow = tables()
    hbm = pl.BlockSpec(memory_space=pltpu.HBM)
    vmem = pltpu.VMEM
    dma = pltpu.SemaphoreType.DMA
    edges = [(2, 4, LX, LANES), (2, 4, LY, LANES)]
    parts = pl.pallas_call(
        kernel,
        out_shape=[jax.ShapeDtypeStruct(s, F32) for s in [field_now.shape] + edges],
        in_specs=[hbm] * 3 + [pl.BlockSpec(memory_space=pltpu.SMEM)] + [hbm] * 2,
        out_specs=[hbm] * 3,
        scratch_shapes=[
            vmem((4, PAD_X, PAD_Y, LANES), F32),
            vmem((4, PAD_X, PAD_Y, LANES), F32),
            vmem(field_now.shape, F32),
            vmem(edges[0], F32),
            vmem(edges[1], F32),
            vmem((4, LX, LY, LANES), F32),
            vmem((2, LX, LY, LANES), F32),
            vmem((2, LX, LY, LANES), F32),
            vmem((LX, LY, LANES), F32),
            vmem((4, CX * LY, LANES), F32),
            vmem((4, CX * CY, LANES), F32),
            vmem(wide.shape, F32),
            vmem(narrow.shape, F32),
        ] + [vmem((DEVICES, 4, LANES), F32)] * 4 + [
            vmem((3, 2, 4, LX, LANES), F32),
            vmem((3, 2, 4, LY, LANES), F32),
            vmem((3, 2, 4, LX, LANES), F32),
            vmem((3, 2, 4, LY, LANES), F32),
            vmem((2, 2, 4, CX, LANES), F32),
            vmem((2, 2, 4, CY, LANES), F32),
            vmem((2, 2, 4, CX, LANES), F32),
            vmem((2, 2, 4, CY, LANES), F32),
            dma((4,)),
            dma((PARTS, 6)),
            dma((2,)),
            dma((4,)),
            dma((5, 4)),
            dma((5, 4)),
            dma((PARTS, 2)),
            pltpu.SemaphoreType.REGULAR,
        ],
        compiler_params=pltpu.CompilerParams(
            collective_id=0, has_side_effects=True, vmem_limit_bytes=LIMIT),
        name="schwarz",
    )(field_now, source, wavenumber_sq, shift_sq, wide, narrow)
    return pl.pallas_call(
        finish,
        out_shape=jax.ShapeDtypeStruct(field_now.shape, F32),
        in_specs=[hbm] * 3,
        out_specs=hbm,
        scratch_shapes=[
            vmem(field_now.shape, F32),
            vmem(edges[0], F32),
            vmem(edges[1], F32),
            dma((2, PARTS)),
            dma((2,)),
            dma((2, PARTS)),
        ],
        compiler_params=pltpu.CompilerParams(vmem_limit_bytes=LIMIT),
        name="finish",
    )(*parts)


def solution(mesh):
    return jax.shard_map(
        body,
        mesh=mesh,
        in_specs=(
            P(None, "group", "dev", None),
            P(None, "group", "dev", None),
            P("group", "dev", None),
            P(),
        ),
        out_specs=P(None, "group", "dev", None),
        check_vma=False,
    )
```
